32 devices in a mesh: section: 2 (over x), dp: 4 (over z), mp: 4 (over y, core).
Axes of the slice: x: 2, y: 2, z: 4, core: 2. Of those that a mesh axis runs over, the one named last changes fastest.
Arguments:
- hidden: bfloat16 [2, 512, 4096], P('section', 'dp'), may hold values from -9 to 9
- norm_gain: float32 [2, 4096], P('section'), may hold values from 0.5 to 1.5
- kv_weight: bfloat16 [2, 4096, 2048], P('section', None, 'mp'), may hold values from -1 to 1
- attn_flat: bfloat16 [2, 4, 8388608], P('section', 'mp', 'dp'), may hold values from -1 to 1
- final_gain: float32 [4096], replicated, may hold values from 0.5 to 1.5
- reward_head: float32 [4096], replicated, may hold values from -0.09375 to 0.09375
- segment_ids: int32 [2, 4], P('section'), may hold values from 0 to 2, never falling along the last dimension, each value on 1 to 2 neighbouring positions
- ranks: int32 [2], replicated, may hold values from 0 to 999
Outputs:
- next_hidden: bfloat16 [2, 512, 4096], P('section', 'dp')
- rewards: float32 [2], replicated
- pair_loss: float32 [2, 2], replicated
The draws below stay inside these ranges and needn't reach their ends.
Inputs may be any that keep to these rules, and one draw needn't show every extreme that they name: `segment_ids`: each row's segment numbers never fall, every number of 0 to 2 is present, each on 1 to 2 blocks, one on exactly 2.
All inputs are finite; a program needn't handle non-finite values.
Results may differ from the reference program's by a relative error of at most 0.035.
Values may be sent and summed in bfloat16 or wider, within the bound.
A program may use at most 128 MiB of HBM per device.

```python
import math
import jax
import jax.numpy as jnp
import numpy as np
from jax import lax

D = 4096
HD = 128
QH = 32
KVH = 8
BLK = 128
L = 512
R = 2
MOST = 2
SHARD = 2097152
N_SECTION = 2
N_DP = 4
N_MP = 4


def plant_signs(key):
    shared = jax.random.fold_in(key, 7001)
    sign_key = jax.random.fold_in(shared, 1)
    head_key = jax.random.fold_in(shared, 2)
    direction = (2 * jax.random.randint(sign_key, (D,), 0, 2) - 1).astype(jnp.float32)
    pattern = (2 * jax.random.randint(head_key, (HD,), 0, 2) - 1).astype(jnp.float32)
    return (direction, pattern)


def plant_strength():
    return (332.4 / (D * D * HD ** 0.5)) ** 0.5


def draw_hidden(key, part):
    direction, pattern = plant_signs(key)
    noise_key = jax.random.fold_in(key, 11)
    pick_key = jax.random.fold_in(key, 12)
    level_key = jax.random.fold_in(key, 13)
    first_key = jax.random.fold_in(key, 14)
    full_shape = (N_SECTION, L, D)
    noise_part = jax.random.truncated_normal(noise_key, -6.0, 6.0, full_shape, jnp.float32)
    chance = jax.random.randint(pick_key, (N_SECTION, L), 0, 16)
    position = jnp.arange(L, dtype=jnp.int32)
    in_first = (position < BLK)[None, :]
    forced = position[None, :] == jax.random.randint(first_key, (N_SECTION, 1), 0, BLK)
    planted = jnp.where(in_first, chance < 8, chance == 0) | forced
    level_pick = jnp.where(forced, 2, jax.random.randint(level_key, (N_SECTION, L), 0, 3))
    amount = jnp.where(level_pick == 0, 0.7, jnp.where(level_pick == 1, 1.2, 3.0))
    amount = jnp.where(planted, amount, 0.0)
    return (noise_part + amount[..., None] * direction).astype(jnp.bfloat16)


def draw_kv_weight(key, part):
    direction, pattern = plant_signs(key)
    random_part = jax.random.truncated_normal(jax.random.fold_in(key, 21), -4.0, 4.0, (N_SECTION, D, 2 * KVH * HD), jnp.float32) * D ** (-0.5)
    columns = jnp.stack([pattern, jnp.zeros_like(pattern)], 0).reshape(-1)
    columns = jnp.tile(columns, KVH)
    return (random_part + plant_strength() * direction[:, None] * columns[None, :]).astype(jnp.bfloat16)


def draw_attn_flat(key, part):
    direction, pattern = plant_signs(key)
    query_width = QH * HD // N_MP
    whole_length = N_DP * SHARD
    random_part = jax.random.truncated_normal(jax.random.fold_in(key, 31), -4.0, 4.0, (N_SECTION, N_MP, whole_length), jnp.float32) * D ** (-0.5)
    planted_row = (direction[:, None] * jnp.tile(pattern, query_width // HD)[None, :]).reshape(-1) * plant_strength()
    planted_row = jnp.concatenate([planted_row, jnp.zeros((whole_length - D * query_width,), jnp.float32)])
    return (random_part + planted_row).astype(jnp.bfloat16)


def split_up(number_of, total, limit, lean):
    loads = [(1 << 20) // math.isqrt(standing ** lean) + 1 for standing in range(2, number_of + 1)]
    surplus, given = total - limit - (number_of - 1), [1] * (number_of - 1)
    while surplus > 0:
        movable = [i for i in range(number_of - 1) if given[i] < limit]
        pool, remaining = sum([loads[i] for i in movable]), surplus
        for i in movable:
            extra = min(limit - given[i], max(1, remaining * loads[i] // pool), surplus)
            given[i] = given[i] + extra
            surplus = surplus - extra
    return np.array([limit] + given)


def uneven(stream_key, number_of, total, reach, lean):
    if number_of == 2:
        one = jax.random.randint(stream_key, (), max(1, total - reach), min(reach, total - 1) + 1)
        return jnp.stack([one, total - one])
    lengths = jnp.asarray(split_up(number_of, total, reach, lean), jnp.int32)
    twos = (number_of - 1) // 2
    donor, sink = lengths[1:1 + 2 * twos:2], lengths[2:2 + 2 * twos:2]
    room = jnp.minimum(donor - 1, reach - sink)
    passed = jax.random.randint(jax.random.fold_in(stream_key, 1), (twos,), 0, 1 << 20) % (room + 1)
    lengths = lengths.at[1:1 + 2 * twos:2].set(donor - passed).at[2:2 + 2 * twos:2].set(sink + passed)
    return lengths[jax.random.permutation(jax.random.fold_in(stream_key, 2), number_of)]


def noise(own_key, dims, deviation, most, kind=jnp.bfloat16):
    result = deviation * jax.random.normal(own_key, dims, jnp.float32)
    return jnp.clip(result, min=-most, max=most).astype(kind)


def setup_inputs(seed: int = 0) -> dict:
    arg_keys = jax.random.split(jax.random.key(seed), 9)
    return {
        "hidden": draw_hidden(jax.random.fold_in(arg_keys[8], 71), 0),
        "norm_gain": jnp.clip(1.0 + 0.1 * jax.random.normal(arg_keys[1], (N_SECTION, D), jnp.float32), 0.5, 1.5),
        "kv_weight": draw_kv_weight(jax.random.fold_in(arg_keys[8], 71), 0),
        "attn_flat": draw_attn_flat(jax.random.fold_in(arg_keys[8], 71), 0),
        "final_gain": jnp.clip(1.0 + 0.1 * jax.random.normal(arg_keys[4], (D,), jnp.float32), 0.5, 1.5),
        "reward_head": noise(arg_keys[5], (D,), D ** -0.5, 0.09375, jnp.float32),
        "segment_ids": jax.vmap(lambda own: jnp.searchsorted(jnp.cumsum(uneven(own, R + 1, N_DP, MOST, 0)), jnp.arange(N_DP), side="right"))(jax.random.split(arg_keys[6], N_SECTION)).reshape((N_SECTION, N_DP)).astype(jnp.int32),
        "ranks": jax.random.randint(arg_keys[7], (R,), 0, 1000).astype(jnp.int32),
    }


EPS = 1e-05

def block_attention(query, keyval, seg, kv_local, group):
    length = query.shape[0]
    q_four = query.reshape(length, kv_local, group, HD).astype(jnp.float32)
    pieces = keyval.reshape(length, kv_local, 2, HD).astype(jnp.float32)
    keys = pieces[:, :, 0]
    values = pieces[:, :, 1]
    pos = jnp.arange(length, dtype=jnp.int32)
    blk = pos // BLK
    seg_tok = seg[blk]
    earlier = (blk[None, :] < blk[:, None]) & ((seg_tok[None, :] == 0) | (seg_tok[None, :] == seg_tok[:, None]))
    same = (blk[None, :] == blk[:, None]) & (pos[None, :] <= pos[:, None])
    visible = earlier | same
    scores = jnp.einsum('tjgd,cjd->jgtc', q_four, keys) * HD ** (-0.5)
    scores = jnp.where(visible[None, None], scores, -1e+30)
    peak = lax.optimization_barrier(jnp.max(scores, -1, keepdims=True))
    weights = jnp.where(visible[None, None], jnp.exp(scores - peak), 0.0)
    total = lax.optimization_barrier(jnp.sum(weights, -1))
    rounded = lax.optimization_barrier(weights.astype(jnp.bfloat16)).astype(jnp.float32)
    mixed = jnp.einsum('jgtc,cjd->jgtd', rounded, values) / total[..., None]
    return mixed.transpose(2, 0, 1, 3).reshape(length, kv_local * group * HD).astype(jnp.bfloat16)

def reference(hidden, norm_gain, kv_weight, attn_flat, final_gain, reward_head, segment_ids, ranks):
    kv_local = KVH // N_MP
    group = QH // KVH
    q_width = kv_local * group * HD
    kv_width = 2 * kv_local * HD
    outputs = []
    for phase in range(N_SECTION):
        state = hidden[phase].astype(jnp.float32)
        normed = (state * lax.rsqrt(lax.optimization_barrier(jnp.mean(state * state, -1, keepdims=True)) + EPS) * norm_gain[phase]).astype(jnp.bfloat16)
        keyval = jnp.dot(normed, kv_weight[phase], preferred_element_type=jnp.float32).astype(jnp.bfloat16)
        summed = jnp.zeros(state.shape, jnp.float32)
        for lane in range(N_MP):
            flat = attn_flat[phase, lane]
            w_query = flat[:D * q_width].reshape(D, q_width)
            w_out = flat[D * q_width:2 * D * q_width].reshape(q_width, D)
            query = jnp.dot(normed, w_query, preferred_element_type=jnp.float32).astype(jnp.bfloat16)
            mixed = block_attention(query, keyval[:, lane * kv_width:(lane + 1) * kv_width], segment_ids[phase], kv_local, group)
            term = jnp.dot(mixed, w_out, preferred_element_type=jnp.float32)
            summed = summed + lax.optimization_barrier(term.astype(jnp.bfloat16)).astype(jnp.float32)
        outputs.append((state + summed).astype(jnp.bfloat16))
    next_hidden = jnp.stack([jnp.zeros_like(outputs[0])] + outputs[:-1])
    final = outputs[-1].astype(jnp.float32)
    seg = segment_ids[N_SECTION - 1]
    ends = lax.optimization_barrier(jnp.sum((seg[None, :] <= jnp.arange(1, R + 1, dtype=jnp.int32)[:, None]).astype(jnp.int32), 1)) - 1
    rows = final[(ends + 1) * BLK - 1]
    rewards = lax.optimization_barrier(jnp.sum(rows * final_gain * reward_head, -1)) * lax.rsqrt(lax.optimization_barrier(jnp.mean(rows * rows, -1)) + EPS)
    pair_loss = jnp.where(ranks[:, None] < ranks[None, :], jax.nn.softplus(rewards[None, :] - rewards[:, None]), 0.0)
    return (next_hidden, rewards, pair_loss)
```

```python
import functools

import jax
import jax.numpy as jnp
from jax import lax
from jax.experimental import pallas as pl
from jax.experimental.pallas import tpu as pltpu
from jax.sharding import PartitionSpec as P

HD = 128
QH = 32
KVH = 8


EPS = 1e-05


def passed_along(block, axis, distance):
    devices = range(lax.axis_size(axis))
    route = [(i - distance, i) for i in devices if i - distance in devices]
    return lax.ppermute(block, axis, route)


def gathered_shards(hidden, norm_gain, kv_weight, attn_flat, final_gain, reward_head, segment_ids, ranks):
    state = hidden[0]
    tokens = state.shape[0]
    width = state.shape[1]
    seg_row = segment_ids[0]
    blocks = lax.axis_size("dp")
    block = lax.axis_index("dp")
    phases = lax.axis_size("section")
    phase_now = lax.axis_index("section")
    responses = ranks.shape[0]
    state_wide = state.astype(jnp.float32)
    normed = (
        state_wide
        * lax.rsqrt(jnp.mean(state_wide * state_wide, -1, keepdims=True) + EPS)
        * norm_gain[0]
    ).astype(jnp.bfloat16)
    keyval = jnp.dot(normed, kv_weight[0], preferred_element_type=jnp.float32).astype(jnp.bfloat16)
    kv_local = keyval.shape[1] // (2 * HD)
    group = QH // KVH
    q_width = kv_local * group * HD
    flat = lax.all_gather(attn_flat[0, 0], "dp", axis=0, tiled=True)
    w_query = flat[: width * q_width].reshape(width, q_width)
    w_out = flat[width * q_width : 2 * width * q_width].reshape(q_width, width)
    query = jnp.dot(normed, w_query, preferred_element_type=jnp.float32).astype(jnp.bfloat16)
    query = query.reshape(tokens, kv_local, group, HD)
    block_ids = jnp.arange(blocks, dtype=jnp.int32)
    own_seg = jnp.sum(jnp.where(block_ids == block, seg_row, 0))
    query_pos = block * tokens + jnp.arange(tokens, dtype=jnp.int32)
    piece = lax.all_gather(keyval, "dp", axis=0, tiled=True)
    peak = jnp.full((kv_local, group, tokens), -1e30, jnp.float32)
    count = piece.shape[0]
    key_pos = jnp.arange(count, dtype=jnp.int32)
    key_block = key_pos // tokens
    key_seg = jnp.sum(jnp.where(key_block[:, None] == block_ids[None, :], seg_row[None, :], 0), 1)
    parts = piece.reshape(count, kv_local, 2, HD)
    keys = parts[:, :, 0]
    values = parts[:, :, 1]
    earlier = (key_block < block) & (key_block >= 0) & ((key_seg == 0) | (key_seg == own_seg))
    same = (key_block == block)[None, :] & (key_pos[None, :] <= query_pos[:, None])
    visible = earlier[None, :] | same
    scores = jnp.einsum("tjgd,cjd->jgtc", query, keys, preferred_element_type=jnp.float32) * HD ** (
        -0.5
    )
    scores = jnp.where(visible[None, None], scores, -1e30)
    new_peak = jnp.maximum(peak, jnp.max(scores, -1))
    weights = jnp.where(visible[None, None], jnp.exp(scores - new_peak[..., None]), 0.0)
    total = jnp.sum(weights, -1)
    accum = jnp.einsum(
        "jgtc,cjd->jgtd", weights.astype(jnp.bfloat16), values, preferred_element_type=jnp.float32
    )
    peak, total, accum = (new_peak, total, accum)
    mixed = (
        (accum / total[..., None])
        .transpose(2, 0, 1, 3)
        .reshape(tokens, q_width)
        .astype(jnp.bfloat16)
    )
    partial_value = jnp.dot(mixed, w_out, preferred_element_type=jnp.float32)
    ends = (
        jnp.sum(
            (seg_row[None, :] <= jnp.arange(1, responses + 1, dtype=jnp.int32)[:, None]).astype(
                jnp.int32
            ),
            1,
        )
        - 1
    )
    at_end = (ends == block) & (phase_now == phases - 1)
    summed = lax.psum(partial_value.astype(jnp.bfloat16), "mp").astype(jnp.float32)
    updated = (state_wide + summed).astype(jnp.bfloat16)
    moved = passed_along(updated, "section", 1)
    last_row = updated[tokens - 1].astype(jnp.float32)
    squares = jnp.sum(last_row * last_row)
    product = jnp.sum(last_row * final_gain * reward_head)
    sums_sq, dots = lax.psum(
        (jnp.where(at_end, squares, 0.0), jnp.where(at_end, product, 0.0)), ("section", "dp")
    )
    rewards = dots * lax.rsqrt(sums_sq / width + EPS)
    pair_loss = jnp.where(
        ranks[:, None] < ranks[None, :], jax.nn.softplus(rewards[None, :] - rewards[:, None]), 0.0
    )
    return (moved[None], rewards, pair_loss)


BF = jnp.bfloat16
F32 = jnp.float32
HIDE = -1e30


def copy_to(src, dst, send, recv, **where):
    return pltpu.make_async_remote_copy(
        src_ref=src,
        dst_ref=dst,
        send_sem=send,
        recv_sem=recv,
        device_id=where,
        device_id_type=pl.DeviceIdType.MESH,
    )


def relay_kernel(
    h_ref,
    gain_ref,
    kvw_hbm,
    flat_hbm,
    seg_ref,
    fg_ref,
    rh_ref,
    out_ref,
    stat_ref,
    kvw,
    flat,
    wq,
    wo,
    nrm,
    xq,
    kvs,
    kvr,
    qs,
    qo,
    qr,
    mx,
    mr,
    osend,
    oown,
    orecv,
    ysend,
    yown,
    yrecv,
    zsend,
    zrecv,
    us,
    uin,
    hx,
    hrow,
    qs1,
    qr1,
    osum,
    zin,
    psum,
    pin,
    st,
    sres,
    load_sem,
    adj_s,
    adj_r,
    pair_s,
    pair_r,
    far_s,
    far_r,
    sp_s,
    sp_r,
    row_s,
    row_r,
    kv_s,
    kv_r,
    hx_s,
    hx_r,
    hr_s,
    hr_r,
    w_s,
    w_r,
    p_s,
    p_r,
    q_s,
    q_r,
    m_s,
    m_r,
    o_s,
    o_r,
    y_s,
    y_r,
    z_s,
    z_r,
    u_s,
    u_r,
    f_s,
    f_r,
    st_s,
    st_r,
    sr_s,
    sr_r,
):
    s = lax.axis_index("section")
    d = lax.axis_index("dp")
    m = lax.axis_index("mp")
    y = m // 2
    c = m % 2
    across = (m + 2) % 4
    beside = m + 1 - 2 * c
    first_phase = s == 0
    last_phase = s == 1
    load_kv = pltpu.make_async_copy(kvw_hbm.at[0], kvw, load_sem.at[0])
    CH = 4
    SPAN = 2097152 // CH

    def load_flat(i):
        cut = slice(i * SPAN, (i + 1) * SPAN)
        return pltpu.make_async_copy(
            flat_hbm.at[:, :, cut], flat.at[:, :, cut], load_sem.at[1 + i]
        )

    @pl.when(d >= 2)
    def _():
        load_kv.start()

    for i in range(CH):
        load_flat(i).start()

    @pl.when(d < 2)
    def _():
        load_kv.start()

    barrier = pltpu.get_barrier_semaphore()
    for k in range(1, 4):
        pl.semaphore_signal(
            barrier, inc=1, device_id={"mp": (m + k) % 4}, device_id_type=pl.DeviceIdType.MESH
        )
    for k in range(1, 8):
        t = (s * 4 + d + k) % 8
        pl.semaphore_signal(
            barrier,
            inc=1,
            device_id={"section": t // 4, "dp": t % 4},
            device_id_type=pl.DeviceIdType.MESH,
        )
    h = h_ref[...].astype(F32)
    scale = lax.rsqrt(jnp.mean(h * h, -1, keepdims=True) + EPS)
    nrm[...] = (h * scale * gain_ref[...]).astype(BF)

    mine_out = pl.ds(pl.multiple_of((2 * c + y) * 1024, 1024), 1024)
    across_out = pl.ds(pl.multiple_of((2 * c + 1 - y) * 1024, 1024), 1024)

    natural = pl.ds(pl.multiple_of(m * 1024, 1024), 1024)

    def halves(t):
        return slice(t * 2048, (t + 1) * 2048)

    def keyval():
        load_kv.wait()
        for t in range(2):
            kvs[t] = jnp.dot(
                nrm[...], kvw[:, t * 256 : (t + 1) * 256], preferred_element_type=F32
            ).astype(BF)

            @pl.when(d == t)
            def _():
                kvr[t] = kvs[t]

    def shape_query():
        for i in range(CH):
            load_flat(i).wait()

            @pl.loop(0, 32 // CH)
            def _(k):
                k = k + i * (32 // CH)
                part = flat[0, :, pl.ds(pl.multiple_of(k * 65536, 65536), 65536)].astype(F32)
                wq[pl.ds(pl.multiple_of(k * 64, 64), 64), :] = part.reshape(64, 1024).astype(BF)

    def shape_out():
        for i in range(CH):
            load_flat(i).wait()

            @pl.loop(0, 32 // CH)
            def _(k):
                k = k + i * (32 // CH)
                part = flat[0, :, pl.ds(pl.multiple_of(k * 65536, 65536), 65536)].astype(F32)
                wo[pl.ds(pl.multiple_of(k * 16, 16), 16), :] = part.reshape(16, 4096).astype(BF)

    @pl.when(first_phase)
    def _():
        for t in range(2):

            @pl.when(d == t)
            def _():
                xq[t] = nrm[:, halves(t)]

    @pl.when(last_phase)
    def _():
        for b in range(4):
            for t in range(2):
                if b == t:

                    @pl.when(d == b)
                    def _():
                        xq[0, 16 * b : 16 * b + 16] = nrm[112:128, halves(t)]

    @pl.when(d < 2)
    def _():
        shape_query()

    pl.semaphore_wait(barrier, 10)

    def pair_rows(p):
        return pl.ds(pl.multiple_of(p * 64 + c * 32, 32), 32)

    def adj_send(p):
        rows = pair_rows(p)
        cols = pl.ds(pl.multiple_of((1 - d) * 2048, 2048), 2048)
        return copy_to(
            nrm.at[rows, cols], xq.at[d, rows], adj_s.at[p], adj_r.at[p], dp=1 - d
        )

    def adj_arrive(p):
        rows = pair_rows(p)
        return copy_to(
            xq.at[1 - d, rows], xq.at[1 - d, rows], adj_s.at[p], adj_r.at[p], dp=1 - d
        )

    def pair_copy(p):
        rows = pair_rows(p)
        return copy_to(
            xq.at[1 - d, rows], xq.at[1 - d, rows], pair_s.at[p], pair_r.at[p], mp=beside
        )

    def quarter(p, which):
        return pl.ds(pl.multiple_of(p * 64 + which * 16, 16), 16)

    def far_send(t, p):
        rows = quarter(p, m)
        return copy_to(
            nrm.at[rows, halves(t)],
            xq.at[d, rows],
            far_s.at[t, p],
            far_r.at[d - 2, p],
            dp=t,
        )

    def far_arrive(b, p):
        rows = quarter(p, m)
        return copy_to(
            xq.at[b, rows], xq.at[b, rows], far_s.at[0, p], far_r.at[b - 2, p], dp=b
        )

    def spread(b, p, k):
        rows = quarter(p, across if k == 2 else m)
        return copy_to(
            xq.at[b, rows],
            xq.at[b, rows],
            sp_s.at[b - 2, p, k],
            sp_r.at[b - 2, p, k],
            mp=across if k == 0 else beside,
        )

    def row_send(t):
        return copy_to(
            nrm.at[112:128, halves(t)],
            xq.at[0, pl.ds(pl.multiple_of(d * 16, 16), 16)],
            row_s.at[t],
            row_r.at[d],
            dp=t,
        )

    def row_arrive(b):
        rows = slice(16 * b, 16 * b + 16)
        return copy_to(xq.at[0, rows], xq.at[0, rows], row_s.at[0], row_r.at[b], dp=b)

    def kv_hop(t):
        return copy_to(kvs.at[t], kvr.at[d], kv_s.at[t], kv_r.at[d], dp=t)

    def kv_arrive(b):
        return copy_to(kvr.at[b], kvr.at[b], kv_s.at[0], kv_r.at[b], dp=b)

    def hx_copy():
        return copy_to(h_ref.at[:, mine_out], hx, hx_s, hx_r, section=1 - s)

    def hr_send():
        return copy_to(
            h_ref.at[112:128, natural],
            hrow.at[pl.ds(pl.multiple_of(d * 16, 16), 16)],
            hr_s,
            hr_r.at[d],
            dp=2,
        )

    def hr_arrive(b):
        rows = slice(16 * b, 16 * b + 16)
        return copy_to(hrow.at[rows], hrow.at[rows], hr_s, hr_r.at[b], dp=b)

    @pl.when(first_phase)
    def _():
        @pl.when(d < 2)
        def _():
            for p in range(2):
                adj_send(p).start()

        @pl.when(d >= 2)
        def _():
            for p in range(2):
                for t in (1, 0):
                    far_send(t, p).start()

    @pl.when(last_phase)
    def _():
        for t in range(2):

            @pl.when(d != t)
            def _():
                row_send(t).start()

    keyval()
    for t in range(2):

        @pl.when(d != t)
        def _():
            kv_hop(t).start()

    @pl.when(first_phase)
    def _():
        hx_copy().start()
        out_ref[...] = jnp.zeros_like(out_ref)

    @pl.when(last_phase)
    def _():
        @pl.when(d != 2)
        def _():
            hr_send().start()

        @pl.when(d == 2)
        def _():
            hrow[32:48] = h_ref[112:128, natural]

    def q_copy(g):
        return copy_to(qs.at[g], qr.at[g], q_s.at[g], q_r.at[g], dp=1 - d)

    def m_copy(g):
        return copy_to(mx.at[g], mr.at[g], m_s.at[g], m_r.at[g], dp=d + 2)

    def m_arrive(g):
        return copy_to(mr.at[g], mr.at[g], m_s.at[g], m_r.at[g], dp=d - 2)

    def w_query():
        return copy_to(qs1, qr1, w_s.at[0], w_r.at[0], dp=1 - d)

    def w_out():
        return copy_to(osum, zin, w_s.at[1], w_r.at[1], dp=5 - d)

    def project(g):
        b, rows = g // 2, slice(g % 2 * 64, g % 2 * 64 + 64)
        mine = pl.ds(pl.multiple_of(d * 512, 512), 512)
        other = pl.ds(pl.multiple_of((1 - d) * 512, 512), 512)
        qs[g] = jnp.dot(xq[b, rows], wq[:, other], preferred_element_type=F32).astype(BF)
        q_copy(g).start()
        qo[g] = jnp.dot(xq[b, rows], wq[:, mine], preferred_element_type=F32)

    def attend(g, blocks, mask):
        q_copy(g).wait_recv()
        mix(g, qo[g] + qr[g].astype(F32), blocks, mask)

    def mix(g, q, blocks, mask):
        q = q.astype(BF)
        q = jnp.concatenate([q[:, j * HD : (j + 1) * HD] for j in range(4)], 0)
        scores = []
        for j in range(blocks):
            score = (
                lax.dot_general(
                    q, kvr[j, :, :HD], (((1,), (1,)), ((), ())), preferred_element_type=F32
                )
                * HD ** (-0.5)
            )
            scores.append(mask(j, score))
        peak = functools.reduce(jnp.maximum, [jnp.max(x, -1, keepdims=True) for x in scores])
        total = jnp.zeros_like(peak)
        mixed = jnp.zeros((256, HD), F32)
        for j in range(blocks):
            weight = jnp.exp(scores[j] - peak)
            total = total + jnp.sum(weight, -1, keepdims=True)
            mixed = mixed + jnp.dot(
                weight.astype(BF), kvr[j, :, HD:], preferred_element_type=F32
            )
        mixed = (mixed / total).astype(BF)
        for j in range(4):
            mx[g, :, j * HD : (j + 1) * HD] = mixed[j * 64 : (j + 1) * 64]
        m_copy(g).start()

    def block_mask(g):
        b, half = g // 2, g % 2

        def mask(j, score):
            if j < b:
                seen = (seg_ref[0, j] == 0) | (seg_ref[0, j] == seg_ref[0, b])
                return score + jnp.where(seen, 0.0, HIDE)
            row = lax.broadcasted_iota(jnp.int32, score.shape, 0) % 64 + half * 64
            col = lax.broadcasted_iota(jnp.int32, score.shape, 1)
            return jnp.where(col <= row, score, HIDE)

        return mask

    def ends_mask(j, score):
        row = lax.broadcasted_iota(jnp.int32, score.shape, 0) % 64
        col = lax.broadcasted_iota(jnp.int32, score.shape, 1)
        of = row // 16
        own = jnp.zeros_like(row)
        for b in range(4):
            own = own + jnp.where(of == b, seg_ref[0, b], 0)
        earlier = (of > j) & ((own == seg_ref[0, j]) | (seg_ref[0, j] == 0))
        same = (of == j) & (col <= row % 16 + 112)
        return jnp.where(earlier | same, score, HIDE)

    @pl.when((d < 2) & first_phase)
    def _():
        def adjacent(p):
            adj_arrive(p).wait_recv()
            pair_copy(p).start()

        def joined(p):
            pair_copy(p).wait_recv()

        def receive(b, p):
            far_arrive(b, p).wait_recv()
            spread(b, p, 0).start()
            spread(b, p, 1).start()

        def forward(b, p):
            spread(b, p, 0).wait_recv()
            spread(b, p, 2).start()

        def complete(b, p):
            spread(b, p, 1).wait_recv()
            spread(b, p, 2).wait_recv()

        def keys(b):
            @pl.when(d != b)
            def _():
                kv_arrive(b).wait_recv()

        def paired(g):
            @pl.when(d != g // 2)
            def _():
                joined(g % 2)

        adjacent(0)
        paired(0)
        project(0)
        adjacent(1)
        paired(1)
        project(1)
        keys(0)
        attend(0, 1, block_mask(0))
        paired(2)
        project(2)
        receive(2, 0)
        attend(1, 1, block_mask(1))
        receive(2, 1)
        paired(3)
        project(3)
        keys(1)
        forward(2, 0)
        attend(2, 2, block_mask(2))
        forward(2, 1)
        complete(2, 0)
        project(4)
        receive(3, 0)
        attend(3, 2, block_mask(3))
        receive(3, 1)
        complete(2, 1)
        project(5)
        forward(3, 0)
        keys(2)
        attend(4, 3, block_mask(4))
        forward(3, 1)
        complete(3, 0)
        project(6)
        attend(5, 3, block_mask(5))
        complete(3, 1)
        project(7)
        keys(3)
        attend(6, 4, block_mask(6))
        attend(7, 4, block_mask(7))

    @pl.when((d < 2) & last_phase)
    def _():
        for b in range(4):

            @pl.when(d != b)
            def _():
                row_arrive(b).wait_recv()

        mine = pl.ds(pl.multiple_of(d * 512, 512), 512)
        other = pl.ds(pl.multiple_of((1 - d) * 512, 512), 512)
        qs1[...] = jnp.dot(xq[0, 0:64], wq[:, other], preferred_element_type=F32)
        w_query().start()
        own = jnp.dot(xq[0, 0:64], wq[:, mine], preferred_element_type=F32)
        for b in range(4):

            @pl.when(d != b)
            def _():
                kv_arrive(b).wait_recv()

        w_query().wait_recv()
        mix(0, own + qr1[...], 4, ends_mask)

    def o_copy(g):
        return copy_to(osend.at[g], orecv.at[g], o_s.at[g], o_r.at[g], mp=beside)

    def y_copy(g):
        return copy_to(ysend.at[g], yrecv.at[g], y_s.at[g], y_r.at[g], mp=across)

    def z_copy(g):
        return copy_to(zsend.at[g], zrecv.at[g], z_s.at[g], z_r.at[g], dp=5 - d)

    def u_copy(g):
        return pltpu.make_async_remote_copy(
            src_ref=us.at[g],
            dst_ref=uin.at[g % 2],
            send_sem=u_s.at[g],
            recv_sem=u_r.at[g % 2],
            device_id={"section": 1, "dp": g // 2},
            device_id_type=pl.DeviceIdType.MESH,
        )

    def keeper(g):
        return 3 if g >= 6 else 2

    def first(g):
        m_arrive(g).wait_recv()
        mine = pl.ds(pl.multiple_of(c * 2048, 2048), 2048)
        other = pl.ds(pl.multiple_of((1 - c) * 2048, 2048), 2048)
        osend[g] = jnp.dot(mr[g], wo[:, other], preferred_element_type=F32).astype(BF)
        o_copy(g).start()
        oown[g] = jnp.dot(mr[g], wo[:, mine], preferred_element_type=F32)

    def second(g):
        o_copy(g).wait_recv()
        mine = pl.ds(pl.multiple_of(y * 1024, 1024), 1024)
        other = pl.ds(pl.multiple_of((1 - y) * 1024, 1024), 1024)
        ysend[g] = (oown[g, :, other] + orecv[g, :, other].astype(F32)).astype(BF)
        y_copy(g).start()
        yown[g] = oown[g, :, mine] + orecv[g, :, mine].astype(F32)

    def third(g):
        y_copy(g).wait_recv()

        @pl.when(d != keeper(g))
        def _():
            zsend[g] = (yown[g] + yrecv[g].astype(F32)).astype(BF)
            z_copy(g).start()

        @pl.when(d == keeper(g))
        def _():
            yown[g] = yown[g] + yrecv[g].astype(F32)

    def fourth(g):
        @pl.when(d == keeper(g))
        def _():
            z_copy(g).wait_recv()
            us[g] = (yown[g] + zrecv[g].astype(F32)).astype(BF)
            u_copy(g).start()

    @pl.when(d >= 2)
    def _():
        shape_out()

    @pl.when((d >= 2) & first_phase)
    def _():
        for g in range(12):
            if g < 8:
                first(g)
            if 0 <= g - 2 < 8:
                third(g - 2)
            if 0 <= g - 4 < 8:
                fourth(g - 4)
            if g < 8:
                second(g)

    def st_copy(k):
        t = (m + k) % 4
        return copy_to(st.at[m], st.at[m], st_s.at[k - 1], st_r.at[k - 1], mp=t)

    def st_arrive(k):
        t = (m + 4 - k) % 4
        return copy_to(st.at[t], st.at[t], st_s.at[k - 1], st_r.at[k - 1], mp=t)

    def sr_copy(k):
        t = (6 + k) % 8
        return pltpu.make_async_remote_copy(
            src_ref=sres,
            dst_ref=sres,
            send_sem=sr_s.at[k - 1],
            recv_sem=sr_r,
            device_id={"section": t // 4, "dp": t % 4},
            device_id_type=pl.DeviceIdType.MESH,
        )

    def p_copy(k):
        t = (m + k) % 4
        return copy_to(psum.at[t], pin.at[m], p_s.at[k - 1], p_r.at[k - 1], mp=t)

    def p_arrive(k):
        t = (m + 4 - k) % 4
        return copy_to(pin.at[t], pin.at[t], p_s.at[k - 1], p_r.at[k - 1], mp=t)

    def last_rows(a):
        rest = jnp.zeros((4, a.shape[1]), F32)
        return jnp.concatenate([a[16 * b + 15 : 16 * b + 16] for b in range(4)] + [rest], 0)

    @pl.when((d >= 2) & last_phase)
    def _():
        m_arrive(0).wait_recv()
        for k in range(4):
            cols = slice(k * 1024, k * 1024 + 1024)
            osum[:, cols] = last_rows(jnp.dot(mr[0], wo[:, cols], preferred_element_type=F32))

        @pl.when(d == 3)
        def _():
            w_out().start()

    @pl.when((d == 2) & last_phase)
    def _():
        for b in (0, 1, 3):
            hr_arrive(b).wait_recv()
        w_out().wait_recv()
        for k in range(4):
            cols = slice(k * 1024, k * 1024 + 1024)
            psum[k] = (osum[:, cols] + zin[:, cols]).astype(BF).astype(F32)
        pin[m] = psum[m]
        for k in range(1, 4):
            p_copy(k).start()
        for k in range(1, 4):
            p_arrive(k).wait_recv()
        total = (pin[0] + pin[1]) + (pin[2] + pin[3])
        v = (last_rows(hrow[...].astype(F32)) + total).astype(BF).astype(F32)
        squares = jnp.sum(v * v, -1, keepdims=True)
        product = jnp.sum(v * fg_ref[:, natural] * rh_ref[:, natural], -1, keepdims=True)
        spot = lax.broadcasted_iota(jnp.int32, squares.shape, 0)
        half = lax.broadcasted_iota(jnp.int32, (8, 128), 0) < 4
        for r in range(sres.shape[0]):
            end = -1
            for b in range(4):
                end = end + jnp.where(seg_ref[0, b] <= r + 1, 1, 0)
            here = spot == end
            one = jnp.sum(jnp.where(here, squares, 0.0), keepdims=True)
            two = jnp.sum(jnp.where(here, product, 0.0), keepdims=True)
            st[m, r] = jnp.where(half, one, two)
        for k in range(1, 4):
            st_copy(k).start()
        for k in range(1, 4):
            st_arrive(k).wait_recv()
        sres[...] = (st[0] + st[1]) + (st[2] + st[3])
        for k in range(1, 8):
            sr_copy(k).start()

    @pl.when(last_phase)
    def _():
        def f_copy(p, k):
            rows = slice(p * 64, p * 64 + 64)
            cols = across_out if k == 2 else mine_out
            return copy_to(
                out_ref.at[rows, cols],
                out_ref.at[rows, cols],
                f_s.at[p, k],
                f_r.at[p, k],
                mp=across if k == 0 else beside,
            )

        def u_arrive(p):
            return copy_to(uin.at[p], uin.at[p], u_s.at[p], u_r.at[p], section=0)

        copy_to(hx, hx, hx_s, hx_r, section=0).wait_recv()
        for p in range(2):
            rows = slice(p * 64, p * 64 + 64)
            u_arrive(p).wait_recv()
            out_ref[rows, mine_out] = (
                hx[rows].astype(F32) + uin[p].astype(F32)
            ).astype(BF)
            f_copy(p, 0).start()
            f_copy(p, 1).start()
        for p in range(2):
            f_copy(p, 0).wait_recv()
            f_copy(p, 2).start()
        for p in range(2):
            f_copy(p, 1).wait_recv()
            f_copy(p, 2).wait_recv()
        for p in range(2):
            for k in range(3):
                f_copy(p, k).wait_send()

    leader = (d == 2) & last_phase

    @pl.when(jnp.logical_not(leader))
    def _():
        sr_copy(1).wait_recv()

    stat_ref[...] = sres[...]

    @pl.when(leader)
    def _():
        for k in range(1, 4):
            st_copy(k).wait_send()
        for k in range(1, 8):
            sr_copy(k).wait_send()

    for t in range(2):

        @pl.when(d != t)
        def _():
            kv_hop(t).wait_send()

            @pl.when(last_phase)
            def _():
                row_send(t).wait_send()

    @pl.when(first_phase)
    def _():
        hx_copy().wait_send()

        @pl.when(d < 2)
        def _():
            for p in range(2):
                adj_send(p).wait_send()
                pair_copy(p).wait_send()
                for b in (2, 3):
                    for k in range(3):
                        spread(b, p, k).wait_send()
            for g in range(8):
                q_copy(g).wait_send()
                m_copy(g).wait_send()

        @pl.when(d >= 2)
        def _():
            for p in range(2):
                for t in range(2):
                    far_send(t, p).wait_send()
            for g in range(8):
                o_copy(g).wait_send()
                y_copy(g).wait_send()

                @pl.when(d != keeper(g))
                def _():
                    z_copy(g).wait_send()

                @pl.when(d == keeper(g))
                def _():
                    u_copy(g).wait_send()

    @pl.when(last_phase)
    def _():
        @pl.when(d != 2)
        def _():
            hr_send().wait_send()

        @pl.when(d < 2)
        def _():
            w_query().wait_send()
            m_copy(0).wait_send()

        @pl.when(d == 3)
        def _():
            w_out().wait_send()

        @pl.when(d == 2)
        def _():
            for k in range(1, 4):
                p_copy(k).wait_send()


def kept_shards(hidden, norm_gain, kv_weight, attn_flat, final_gain, reward_head, segment_ids, ranks):
    width = hidden.shape[2]
    responses = ranks.shape[0]
    vmem = pl.BlockSpec(memory_space=pltpu.VMEM)
    anywhere = pl.BlockSpec(memory_space=pl.ANY)
    dma = pltpu.SemaphoreType.DMA
    V = pltpu.VMEM
    moved, stats = pl.pallas_call(
        relay_kernel,
        out_shape=(
            jax.ShapeDtypeStruct((128, 4096), BF),
            jax.ShapeDtypeStruct((responses, 8, 128), F32),
        ),
        in_specs=[
            vmem,
            vmem,
            anywhere,
            anywhere,
            pl.BlockSpec(memory_space=pltpu.SMEM),
            vmem,
            vmem,
        ],
        out_specs=(vmem, vmem),
        scratch_shapes=[
            V((4096, 512), BF),
            V((1, 1, 2097152), BF),
            V((2048, 1024), BF),
            V((512, 4096), BF),
            V((128, 4096), BF),
            V((4, 128, 2048), BF),
            V((2, 128, 256), BF),
            V((4, 128, 256), BF),
            V((8, 64, 512), BF),
            V((8, 64, 512), F32),
            V((8, 64, 512), BF),
            V((8, 64, 512), BF),
            V((8, 64, 512), BF),
            V((8, 64, 2048), BF),
            V((8, 64, 2048), F32),
            V((8, 64, 2048), BF),
            V((8, 64, 1024), BF),
            V((8, 64, 1024), F32),
            V((8, 64, 1024), BF),
            V((8, 64, 1024), BF),
            V((8, 64, 1024), BF),
            V((8, 64, 1024), BF),
            V((2, 64, 1024), BF),
            V((128, 1024), BF),
            V((64, 1024), BF),
            V((64, 512), F32),
            V((64, 512), F32),
            V((8, 4096), F32),
            V((8, 4096), F32),
            V((4, 8, 1024), F32),
            V((4, 8, 1024), F32),
            V((4, responses, 8, 128), F32),
            V((responses, 8, 128), F32),
            dma((5,)),
            dma((2,)),
            dma((2,)),
            dma((2,)),
            dma((2,)),
            dma((2, 2)),
            dma((2, 2)),
            dma((2, 2, 3)),
            dma((2, 2, 3)),
            dma((2,)),
            dma((4,)),
            dma((2,)),
            dma((4,)),
            dma(()),
            dma(()),
            dma(()),
            dma((4,)),
            dma((2,)),
            dma((2,)),
            dma((3,)),
            dma((3,)),
            dma((8,)),
            dma((8,)),
            dma((8,)),
            dma((8,)),
            dma((8,)),
            dma((8,)),
            dma((8,)),
            dma((8,)),
            dma((8,)),
            dma((8,)),
            dma((8,)),
            dma((2,)),
            dma((2, 3)),
            dma((2, 3)),
            dma((3,)),
            dma((3,)),
            dma((7,)),
            dma(()),
        ],
        compiler_params=pltpu.CompilerParams(
            collective_id=0, has_side_effects=True, vmem_limit_bytes=60 << 20
        ),
    )(
        hidden[0],
        norm_gain,
        kv_weight,
        attn_flat,
        segment_ids,
        final_gain[None],
        reward_head[None],
    )
    rewards = stats[:, 4, 0] * lax.rsqrt(stats[:, 0, 0] / width + EPS)
    pair_loss = jnp.where(
        ranks[:, None] < ranks[None, :], jax.nn.softplus(rewards[None, :] - rewards[:, None]), 0.0
    )
    return (moved[None], rewards, pair_loss)


def shards(hidden, norm_gain, kv_weight, attn_flat, final_gain, reward_head, segment_ids, ranks):
    blocks = lax.axis_size("dp")
    lanes = lax.axis_size("mp")
    kv_local = kv_weight.shape[2] // (2 * HD)
    kept = (
        (lax.axis_size("section"), blocks, lanes, kv_local) == (2, 4, 4, 2)
        and hidden.shape[1:] == (128, 4096)
        and attn_flat.shape == (1, 1, 2097152)
    )
    args = (hidden, norm_gain, kv_weight, attn_flat, final_gain, reward_head, segment_ids, ranks)
    return (kept_shards if kept else gathered_shards)(*args)


def solution(mesh):
    placed = (
        P("section", "dp", None),
        P("section", None),
        P("section", None, "mp"),
        P("section", "mp", "dp"),
        P(),
        P(),
        P("section", None),
        P(),
    )
    return jax.shard_map(
        shards,
        mesh=mesh,
        in_specs=placed,
        out_specs=(P("section", "dp", None), P(), P()),
        check_vma=False,
    )
```

```python
import functools

import jax
import jax.numpy as jnp
from jax import lax
from jax.experimental import pallas as pl
from jax.experimental.pallas import tpu as pltpu
from jax.sharding import PartitionSpec as P

HD = 128
QH = 32
KVH = 8


EPS = 1e-05


def passed_along(block, axis, distance):
    devices = range(lax.axis_size(axis))
    route = [(i - distance, i) for i in devices if i - distance in devices]
    return lax.ppermute(block, axis, route)


def gathered_shards(hidden, norm_gain, kv_weight, attn_flat, final_gain, reward_head, segment_ids, ranks):
    state = hidden[0]
    tokens = state.shape[0]
    width = state.shape[1]
    seg_row = segment_ids[0]
    blocks = lax.axis_size("dp")
    block = lax.axis_index("dp")
    phases = lax.axis_size("section")
    phase_now = lax.axis_index("section")
    responses = ranks.shape[0]
    state_wide = state.astype(jnp.float32)
    normed = (
        state_wide
        * lax.rsqrt(jnp.mean(state_wide * state_wide, -1, keepdims=True) + EPS)
        * norm_gain[0]
    ).astype(jnp.bfloat16)
    keyval = jnp.dot(normed, kv_weight[0], preferred_element_type=jnp.float32).astype(jnp.bfloat16)
    kv_local = keyval.shape[1] // (2 * HD)
    group = QH // KVH
    q_width = kv_local * group * HD
    flat = lax.all_gather(attn_flat[0, 0], "dp", axis=0, tiled=True)
    w_query = flat[: width * q_width].reshape(width, q_width)
    w_out = flat[width * q_width : 2 * width * q_width].reshape(q_width, width)
    query = jnp.dot(normed, w_query, preferred_element_type=jnp.float32).astype(jnp.bfloat16)
    query = query.reshape(tokens, kv_local, group, HD)
    block_ids = jnp.arange(blocks, dtype=jnp.int32)
    own_seg = jnp.sum(jnp.where(block_ids == block, seg_row, 0))
    query_pos = block * tokens + jnp.arange(tokens, dtype=jnp.int32)
    piece = lax.all_gather(keyval, "dp", axis=0, tiled=True)
    peak = jnp.full((kv_local, group, tokens), -1e30, jnp.float32)
    count = piece.shape[0]
    key_pos = jnp.arange(count, dtype=jnp.int32)
    key_block = key_pos // tokens
    key_seg = jnp.sum(jnp.where(key_block[:, None] == block_ids[None, :], seg_row[None, :], 0), 1)
    parts = piece.reshape(count, kv_local, 2, HD)
    keys = parts[:, :, 0]
    values = parts[:, :, 1]
    earlier = (key_block < block) & (key_block >= 0) & ((key_seg == 0) | (key_seg == own_seg))
    same = (key_block == block)[None, :] & (key_pos[None, :] <= query_pos[:, None])
    visible = earlier[None, :] | same
    scores = jnp.einsum("tjgd,cjd->jgtc", query, keys, preferred_element_type=jnp.float32) * HD ** (
        -0.5
    )
    scores = jnp.where(visible[None, None], scores, -1e30)
    new_peak = jnp.maximum(peak, jnp.max(scores, -1))
    weights = jnp.where(visible[None, None], jnp.exp(scores - new_peak[..., None]), 0.0)
    total = jnp.sum(weights, -1)
    accum = jnp.einsum(
        "jgtc,cjd->jgtd", weights.astype(jnp.bfloat16), values, preferred_element_type=jnp.float32
    )
    peak, total, accum = (new_peak, total, accum)
    mixed = (
        (accum / total[..., None])
        .transpose(2, 0, 1, 3)
        .reshape(tokens, q_width)
        .astype(jnp.bfloat16)
    )
    partial_value = jnp.dot(mixed, w_out, preferred_element_type=jnp.float32)
    ends = (
        jnp.sum(
            (seg_row[None, :] <= jnp.arange(1, responses + 1, dtype=jnp.int32)[:, None]).astype(
                jnp.int32
            ),
            1,
        )
        - 1
    )
    at_end = (ends == block) & (phase_now == phases - 1)
    summed = lax.psum(partial_value.astype(jnp.bfloat16), "mp").astype(jnp.float32)
    updated = (state_wide + summed).astype(jnp.bfloat16)
    moved = passed_along(updated, "section", 1)
    last_row = updated[tokens - 1].astype(jnp.float32)
    squares = jnp.sum(last_row * last_row)
    product = jnp.sum(last_row * final_gain * reward_head)
    sums_sq, dots = lax.psum(
        (jnp.where(at_end, squares, 0.0), jnp.where(at_end, product, 0.0)), ("section", "dp")
    )
    rewards = dots * lax.rsqrt(sums_sq / width + EPS)
    pair_loss = jnp.where(
        ranks[:, None] < ranks[None, :], jax.nn.softplus(rewards[None, :] - rewards[:, None]), 0.0
    )
    return (moved[None], rewards, pair_loss)


BF = jnp.bfloat16
F32 = jnp.float32
HIDE = -1e30


def copy_to(src, dst, send, recv, **where):
    return pltpu.make_async_remote_copy(
        src_ref=src,
        dst_ref=dst,
        send_sem=send,
        recv_sem=recv,
        device_id=where,
        device_id_type=pl.DeviceIdType.MESH,
    )


def relay_kernel(
    h_ref,
    gain_ref,
    kvw_hbm,
    flat_hbm,
    seg_ref,
    fg_ref,
    rh_ref,
    out_ref,
    stat_ref,
    kvw,
    flat,
    wq,
    wo,
    nrm,
    xq,
    kvs,
    kvr,
    qs,
    qo,
    qr,
    mx,
    mr,
    osend,
    oown,
    orecv,
    ysend,
    yown,
    yrecv,
    zsend,
    zrecv,
    us,
    uin,
    hx,
    hrow,
    rx,
    rkv,
    qs1,
    qr1,
    osum,
    zin,
    psum,
    pin,
    st,
    sres,
    load_sem,
    adj_s,
    adj_r,
    pair_s,
    pair_r,
    far_s,
    far_r,
    sp_s,
    sp_r,
    row_s,
    row_r,
    kv_s,
    kv_r,
    hx_s,
    hx_r,
    hr_s,
    hr_r,
    rx_s,
    rx_r,
    rl_s,
    kx_s,
    kx_r,
    rk_s,
    w_s,
    w_r,
    p_s,
    p_r,
    q_s,
    q_r,
    m_s,
    m_r,
    o_s,
    o_r,
    y_s,
    y_r,
    z_s,
    z_r,
    u_s,
    u_r,
    f_s,
    f_r,
    st_s,
    st_r,
    sr_s,
    sr_r,
):
    s = lax.axis_index("section")
    d = lax.axis_index("dp")
    m = lax.axis_index("mp")
    y = m // 2
    c = m % 2
    across = (m + 2) % 4
    beside = m + 1 - 2 * c
    first_phase = s == 0
    last_phase = s == 1
    load_kv = pltpu.make_async_copy(kvw_hbm.at[0], kvw, load_sem.at[0])
    CH = 4
    SPAN = 2097152 // CH

    def load_flat(i):
        cut = slice(i * SPAN, (i + 1) * SPAN)
        return pltpu.make_async_copy(
            flat_hbm.at[:, :, cut], flat.at[:, :, cut], load_sem.at[1 + i]
        )

    @pl.when(d >= 2)
    def _():
        load_kv.start()

    for i in range(CH):
        load_flat(i).start()

    @pl.when(d < 2)
    def _():
        load_kv.start()

    barrier = pltpu.get_barrier_semaphore()
    for k in range(1, 4):
        pl.semaphore_signal(
            barrier, inc=1, device_id={"mp": (m + k) % 4}, device_id_type=pl.DeviceIdType.MESH
        )
    for k in range(1, 8):
        t = (s * 4 + d + k) % 8
        pl.semaphore_signal(
            barrier,
            inc=1,
            device_id={"section": t // 4, "dp": t % 4},
            device_id_type=pl.DeviceIdType.MESH,
        )
    h = h_ref[...].astype(F32)
    scale = lax.rsqrt(jnp.mean(h * h, -1, keepdims=True) + EPS)
    nrm[...] = (h * scale * gain_ref[...]).astype(BF)

    mine_out = pl.ds(pl.multiple_of((2 * c + y) * 1024, 1024), 1024)
    across_out = pl.ds(pl.multiple_of((2 * c + 1 - y) * 1024, 1024), 1024)

    natural = pl.ds(pl.multiple_of(m * 1024, 1024), 1024)

    def halves(t):
        return slice(t * 2048, (t + 1) * 2048)

    def keyval():
        load_kv.wait()
        for t in range(2):
            kvs[t] = jnp.dot(
                nrm[...], kvw[:, t * 256 : (t + 1) * 256], preferred_element_type=F32
            ).astype(BF)

            @pl.when(d == t)
            def _():
                kvr[t] = kvs[t]

    def shape_query():
        for i in range(CH):
            load_flat(i).wait()

            @pl.loop(0, 32 // CH)
            def _(k):
                k = k + i * (32 // CH)
                part = flat[0, :, pl.ds(pl.multiple_of(k * 65536, 65536), 65536)].astype(F32)
                wq[pl.ds(pl.multiple_of(k * 64, 64), 64), :] = part.reshape(64, 1024).astype(BF)

    def shape_out():
        for i in range(CH):
            load_flat(i).wait()

            @pl.loop(0, 32 // CH)
            def _(k):
                k = k + i * (32 // CH)
                part = flat[0, :, pl.ds(pl.multiple_of(k * 65536, 65536), 65536)].astype(F32)
                wo[pl.ds(pl.multiple_of(k * 16, 16), 16), :] = part.reshape(16, 4096).astype(BF)

    @pl.when(first_phase)
    def _():
        for t in range(2):

            @pl.when(d == t)
            def _():
                xq[t] = nrm[:, halves(t)]

    @pl.when(last_phase)
    def _():
        for b in range(4):
            for t in range(2):
                if b == t:

                    @pl.when(d == b)
                    def _():
                        xq[0, 16 * b : 16 * b + 16] = nrm[112:128, halves(t)]

    @pl.when(d < 2)
    def _():
        shape_query()

    pl.semaphore_wait(barrier, 10)

    def pair_rows(p):
        return pl.ds(pl.multiple_of(p * 64 + c * 32, 32), 32)

    def adj_send(p):
        rows = pair_rows(p)
        cols = pl.ds(pl.multiple_of((1 - d) * 2048, 2048), 2048)
        return copy_to(
            nrm.at[rows, cols], xq.at[d, rows], adj_s.at[p], adj_r.at[p], dp=1 - d
        )

    def adj_arrive(p):
        rows = pair_rows(p)
        return copy_to(
            xq.at[1 - d, rows], xq.at[1 - d, rows], adj_s.at[p], adj_r.at[p], dp=1 - d
        )

    def pair_copy(p):
        rows = pair_rows(p)
        return copy_to(
            xq.at[1 - d, rows], xq.at[1 - d, rows], pair_s.at[p], pair_r.at[p], mp=beside
        )

    def quarter(p, which):
        return pl.ds(pl.multiple_of(p * 64 + which * 16, 16), 16)

    def far_send(p):
        rows = quarter(p, m)
        return copy_to(
            nrm.at[rows, halves(1)], xq.at[d, rows], far_s.at[p], far_r.at[d - 2, p], dp=1
        )

    def far_zero(p):
        rows = quarter(p, m)
        return copy_to(
            nrm.at[rows, halves(0)], xq.at[d, rows], rx_s.at[p], far_r.at[d - 2, p], dp=0
        )

    def x_hop(p):
        return copy_to(
            nrm.at[quarter(p, m), halves(0)], rx.at[p], rx_s.at[p], rx_r.at[p], section=1
        )

    def x_relay(p):
        return pltpu.make_async_remote_copy(
            src_ref=rx.at[p],
            dst_ref=xq.at[d, quarter(p, m)],
            send_sem=rl_s.at[p],
            recv_sem=far_r.at[d - 2, p],
            device_id={"section": 0, "dp": 0},
            device_id_type=pl.DeviceIdType.MESH,
        )

    def kv_x():
        return copy_to(kvs, rkv, kx_s, kx_r, section=1)

    def kv_relay(t):
        return pltpu.make_async_remote_copy(
            src_ref=rkv.at[t],
            dst_ref=kvr.at[d],
            send_sem=rk_s.at[t],
            recv_sem=kv_r.at[d],
            device_id={"section": 0, "dp": t},
            device_id_type=pl.DeviceIdType.MESH,
        )

    def far_arrive(b, p):
        rows = quarter(p, m)
        return copy_to(
            xq.at[b, rows], xq.at[b, rows], far_s.at[p], far_r.at[b - 2, p], dp=b
        )

    def spread(b, p, k):
        rows = quarter(p, across if k == 2 else m)
        return copy_to(
            xq.at[b, rows],
            xq.at[b, rows],
            sp_s.at[b - 2, p, k],
            sp_r.at[b - 2, p, k],
            mp=across if k == 0 else beside,
        )

    def row_send(t):
        return copy_to(
            nrm.at[112:128, halves(t)],
            xq.at[0, pl.ds(pl.multiple_of(d * 16, 16), 16)],
            row_s.at[t],
            row_r.at[d],
            dp=t,
        )

    def row_arrive(b):
        rows = slice(16 * b, 16 * b + 16)
        return copy_to(xq.at[0, rows], xq.at[0, rows], row_s.at[0], row_r.at[b], dp=b)

    def kv_hop(t):
        return copy_to(kvs.at[t], kvr.at[d], kv_s.at[t], kv_r.at[d], dp=t)

    def kv_arrive(b):
        return copy_to(kvr.at[b], kvr.at[b], kv_s.at[0], kv_r.at[b], dp=b)

    def hx_copy():
        return copy_to(h_ref.at[:, mine_out], hx, hx_s, hx_r, section=1 - s)

    def hr_send():
        return copy_to(
            h_ref.at[112:128, natural],
            hrow.at[pl.ds(pl.multiple_of(d * 16, 16), 16)],
            hr_s,
            hr_r.at[d],
            dp=2,
        )

    def hr_arrive(b):
        rows = slice(16 * b, 16 * b + 16)
        return copy_to(hrow.at[rows], hrow.at[rows], hr_s, hr_r.at[b], dp=b)

    @pl.when(first_phase)
    def _():
        @pl.when(d < 2)
        def _():
            for p in range(2):
                adj_send(p).start()

        @pl.when(d >= 2)
        def _():
            for p in range(2):
                far_send(p).start()
                far_zero(p).start()

    @pl.when(last_phase)
    def _():
        for t in range(2):

            @pl.when(d != t)
            def _():
                row_send(t).start()

    keyval()
    hops = (d < 2) | last_phase
    for t in range(2):

        @pl.when(hops & (d != t))
        def _():
            kv_hop(t).start()

    @pl.when((d >= 2) & first_phase)
    def _():
        kv_x().start()

    @pl.when(first_phase)
    def _():
        hx_copy().start()
        out_ref[...] = jnp.zeros_like(out_ref)

    @pl.when(last_phase)
    def _():
        @pl.when(d != 2)
        def _():
            hr_send().start()

        @pl.when(d == 2)
        def _():
            hrow[32:48] = h_ref[112:128, natural]

    def q_copy(g):
        return copy_to(qs.at[g], qr.at[g], q_s.at[g], q_r.at[g], dp=1 - d)

    def m_copy(g):
        return copy_to(mx.at[g], mr.at[g], m_s.at[g], m_r.at[g], dp=d + 2)

    def m_arrive(g):
        return copy_to(mr.at[g], mr.at[g], m_s.at[g], m_r.at[g], dp=d - 2)

    def w_query():
        return copy_to(qs1, qr1, w_s.at[0], w_r.at[0], dp=1 - d)

    def w_out():
        return copy_to(osum, zin, w_s.at[1], w_r.at[1], dp=5 - d)

    def project(g):
        b, rows = g // 2, slice(g % 2 * 64, g % 2 * 64 + 64)
        mine = pl.ds(pl.multiple_of(d * 512, 512), 512)
        other = pl.ds(pl.multiple_of((1 - d) * 512, 512), 512)
        qs[g] = jnp.dot(xq[b, rows], wq[:, other], preferred_element_type=F32).astype(BF)
        q_copy(g).start()
        qo[g] = jnp.dot(xq[b, rows], wq[:, mine], preferred_element_type=F32)

    def attend(g, blocks, mask):
        q_copy(g).wait_recv()
        mix(g, qo[g] + qr[g].astype(F32), blocks, mask)

        m_copy(g).start()

    def mix(g, q, blocks, mask):
        q = q.astype(BF)
        q = jnp.concatenate([q[:, j * HD : (j + 1) * HD] for j in range(4)], 0)
        scores = []
        for j in range(blocks):
            score = (
                lax.dot_general(
                    q, kvr[j, :, :HD], (((1,), (1,)), ((), ())), preferred_element_type=F32
                )
                * HD ** (-0.5)
            )
            scores.append(mask(j, score))
        peak = functools.reduce(jnp.maximum, [jnp.max(x, -1, keepdims=True) for x in scores])
        total = jnp.zeros_like(peak)
        mixed = jnp.zeros((256, HD), F32)
        for j in range(blocks):
            weight = jnp.exp(scores[j] - peak)
            total = total + jnp.sum(weight, -1, keepdims=True)
            mixed = mixed + jnp.dot(
                weight.astype(BF), kvr[j, :, HD:], preferred_element_type=F32
            )
        mixed = (mixed / total).astype(BF)
        for j in range(4):
            mx[g, :, j * HD : (j + 1) * HD] = mixed[j * 64 : (j + 1) * 64]

    def block_mask(g):
        b, half = g // 2, g % 2

        def mask(j, score):
            if j < b:
                seen = (seg_ref[0, j] == 0) | (seg_ref[0, j] == seg_ref[0, b])
                return score + jnp.where(seen, 0.0, HIDE)
            row = lax.broadcasted_iota(jnp.int32, score.shape, 0) % 64 + half * 64
            col = lax.broadcasted_iota(jnp.int32, score.shape, 1)
            return jnp.where(col <= row, score, HIDE)

        return mask

    def ends_mask(j, score):
        row = lax.broadcasted_iota(jnp.int32, score.shape, 0) % 64
        col = lax.broadcasted_iota(jnp.int32, score.shape, 1)
        of = row // 16
        own = jnp.zeros_like(row)
        for b in range(4):
            own = own + jnp.where(of == b, seg_ref[0, b], 0)
        earlier = (of > j) & ((own == seg_ref[0, j]) | (seg_ref[0, j] == 0))
        same = (of == j) & (col <= row % 16 + 112)
        return jnp.where(earlier | same, score, HIDE)

    @pl.when((d < 2) & first_phase)
    def _():
        def adjacent(p):
            adj_arrive(p).wait_recv()
            pair_copy(p).start()

        def joined(p):
            pair_copy(p).wait_recv()

        def receive(b, p):
            far_arrive(b, p).wait_recv()
            spread(b, p, 0).start()
            spread(b, p, 1).start()

        def forward(b, p):
            spread(b, p, 0).wait_recv()
            spread(b, p, 2).start()

        def complete(b, p):
            spread(b, p, 1).wait_recv()
            spread(b, p, 2).wait_recv()

        def keys(b):
            @pl.when(d != b)
            def _():
                kv_arrive(b).wait_recv()

        def paired(g):
            @pl.when(d != g // 2)
            def _():
                joined(g % 2)

        adjacent(0)
        paired(0)
        project(0)
        adjacent(1)
        paired(1)
        project(1)
        keys(0)
        attend(0, 1, block_mask(0))
        paired(2)
        project(2)
        receive(2, 0)
        attend(1, 1, block_mask(1))
        receive(2, 1)
        paired(3)
        project(3)
        keys(1)
        forward(2, 0)
        attend(2, 2, block_mask(2))
        forward(2, 1)
        complete(2, 0)
        project(4)
        receive(3, 0)
        attend(3, 2, block_mask(3))
        receive(3, 1)
        complete(2, 1)
        project(5)
        forward(3, 0)
        keys(2)
        attend(4, 3, block_mask(4))
        forward(3, 1)
        complete(3, 0)
        project(6)
        attend(5, 3, block_mask(5))
        complete(3, 1)
        project(7)
        keys(3)
        attend(6, 4, block_mask(6))
        attend(7, 4, block_mask(7))

    @pl.when((d < 2) & last_phase)
    def _():
        for b in range(4):

            @pl.when(d != b)
            def _():
                row_arrive(b).wait_recv()

        mine = pl.ds(pl.multiple_of(d * 512, 512), 512)
        other = pl.ds(pl.multiple_of((1 - d) * 512, 512), 512)
        qs1[...] = jnp.dot(xq[0, 0:64], wq[:, other], preferred_element_type=F32)
        w_query().start()
        own = jnp.dot(xq[0, 0:64], wq[:, mine], preferred_element_type=F32)
        for b in range(4):

            @pl.when(d != b)
            def _():
                kv_arrive(b).wait_recv()

        w_query().wait_recv()
        mix(0, own + qr1[...], 4, ends_mask)
        m_copy(0).start()

    def o_copy(g):
        return copy_to(osend.at[g], orecv.at[g], o_s.at[g], o_r.at[g], mp=beside)

    def y_copy(g):
        return copy_to(ysend.at[g], yrecv.at[g], y_s.at[g], y_r.at[g], mp=across)

    def z_copy(g):
        return copy_to(zsend.at[g], zrecv.at[g], z_s.at[g], z_r.at[g], dp=5 - d)

    def u_copy(g):
        return pltpu.make_async_remote_copy(
            src_ref=us.at[g],
            dst_ref=uin.at[g % 2],
            send_sem=u_s.at[g],
            recv_sem=u_r.at[g % 2],
            device_id={"section": 1, "dp": g // 2},
            device_id_type=pl.DeviceIdType.MESH,
        )

    def keeper(g):
        return 3 if g >= 6 else 2

    def first(g):
        m_arrive(g).wait_recv()
        mine = pl.ds(pl.multiple_of(c * 2048, 2048), 2048)
        other = pl.ds(pl.multiple_of((1 - c) * 2048, 2048), 2048)
        osend[g] = jnp.dot(mr[g], wo[:, other], preferred_element_type=F32).astype(BF)
        o_copy(g).start()
        oown[g] = jnp.dot(mr[g], wo[:, mine], preferred_element_type=F32)

    def second(g):
        o_copy(g).wait_recv()
        mine = pl.ds(pl.multiple_of(y * 1024, 1024), 1024)
        other = pl.ds(pl.multiple_of((1 - y) * 1024, 1024), 1024)
        ysend[g] = (oown[g, :, other] + orecv[g, :, other].astype(F32)).astype(BF)
        y_copy(g).start()
        yown[g] = oown[g, :, mine] + orecv[g, :, mine].astype(F32)

    def third(g):
        y_copy(g).wait_recv()

        @pl.when(d != keeper(g))
        def _():
            zsend[g] = (yown[g] + yrecv[g].astype(F32)).astype(BF)
            z_copy(g).start()

        @pl.when(d == keeper(g))
        def _():
            yown[g] = yown[g] + yrecv[g].astype(F32)

    def fourth(g):
        @pl.when(d == keeper(g))
        def _():
            z_copy(g).wait_recv()
            us[g] = (yown[g] + zrecv[g].astype(F32)).astype(BF)
            u_copy(g).start()

    @pl.when((d >= 2) & last_phase)
    def _():
        copy_to(rkv, rkv, kx_s, kx_r, section=0).wait_recv()
        for t in (1, 0):
            kv_relay(t).start()

    @pl.when(d >= 2)
    def _():
        shape_out()

    @pl.when((d >= 2) & first_phase)
    def _():
        for g in range(12):
            if g < 8:
                first(g)
            if 0 <= g - 2 < 8:
                third(g - 2)
            if 0 <= g - 4 < 8:
                fourth(g - 4)
            if g < 8:
                second(g)

    def st_copy(k):
        t = (m + k) % 4
        return copy_to(st.at[m], st.at[m], st_s.at[k - 1], st_r.at[k - 1], mp=t)

    def st_arrive(k):
        t = (m + 4 - k) % 4
        return copy_to(st.at[t], st.at[t], st_s.at[k - 1], st_r.at[k - 1], mp=t)

    def sr_copy(k):
        t = (6 + k) % 8
        return pltpu.make_async_remote_copy(
            src_ref=sres,
            dst_ref=sres,
            send_sem=sr_s.at[k - 1],
            recv_sem=sr_r,
            device_id={"section": t // 4, "dp": t % 4},
            device_id_type=pl.DeviceIdType.MESH,
        )

    def p_copy(k):
        t = (m + k) % 4
        return copy_to(psum.at[t], pin.at[m], p_s.at[k - 1], p_r.at[k - 1], mp=t)

    def p_arrive(k):
        t = (m + 4 - k) % 4
        return copy_to(pin.at[t], pin.at[t], p_s.at[k - 1], p_r.at[k - 1], mp=t)

    def last_rows(a):
        rest = jnp.zeros((4, a.shape[1]), F32)
        return jnp.concatenate([a[16 * b + 15 : 16 * b + 16] for b in range(4)] + [rest], 0)

    @pl.when((d >= 2) & last_phase)
    def _():
        m_arrive(0).wait_recv()
        for k in range(4):
            cols = slice(k * 1024, k * 1024 + 1024)
            osum[:, cols] = last_rows(jnp.dot(mr[0], wo[:, cols], preferred_element_type=F32))

        @pl.when(d == 3)
        def _():
            w_out().start()

    @pl.when((d == 2) & last_phase)
    def _():
        for b in (0, 1, 3):
            hr_arrive(b).wait_recv()
        w_out().wait_recv()
        for k in range(4):
            cols = slice(k * 1024, k * 1024 + 1024)
            psum[k] = (osum[:, cols] + zin[:, cols]).astype(BF).astype(F32)
        pin[m] = psum[m]
        for k in range(1, 4):
            p_copy(k).start()
        for k in range(1, 4):
            p_arrive(k).wait_recv()
        total = (pin[0] + pin[1]) + (pin[2] + pin[3])
        v = (last_rows(hrow[...].astype(F32)) + total).astype(BF).astype(F32)
        squares = jnp.sum(v * v, -1, keepdims=True)
        product = jnp.sum(v * fg_ref[:, natural] * rh_ref[:, natural], -1, keepdims=True)
        spot = lax.broadcasted_iota(jnp.int32, squares.shape, 0)
        half = lax.broadcasted_iota(jnp.int32, (8, 128), 0) < 4
        for r in range(sres.shape[0]):
            end = -1
            for b in range(4):
                end = end + jnp.where(seg_ref[0, b] <= r + 1, 1, 0)
            here = spot == end
            one = jnp.sum(jnp.where(here, squares, 0.0), keepdims=True)
            two = jnp.sum(jnp.where(here, product, 0.0), keepdims=True)
            st[m, r] = jnp.where(half, one, two)
        for k in range(1, 4):
            st_copy(k).start()
        for k in range(1, 4):
            st_arrive(k).wait_recv()
        sres[...] = (st[0] + st[1]) + (st[2] + st[3])
        for k in range(1, 8):
            sr_copy(k).start()

    @pl.when(last_phase)
    def _():
        def f_copy(p, k):
            rows = slice(p * 64, p * 64 + 64)
            cols = across_out if k == 2 else mine_out
            return copy_to(
                out_ref.at[rows, cols],
                out_ref.at[rows, cols],
                f_s.at[p, k],
                f_r.at[p, k],
                mp=across if k == 0 else beside,
            )

        def u_arrive(p):
            return copy_to(uin.at[p], uin.at[p], u_s.at[p], u_r.at[p], section=0)

        copy_to(hx, hx, hx_s, hx_r, section=0).wait_recv()
        for p in range(2):
            rows = slice(p * 64, p * 64 + 64)
            u_arrive(p).wait_recv()
            out_ref[rows, mine_out] = (
                hx[rows].astype(F32) + uin[p].astype(F32)
            ).astype(BF)
            f_copy(p, 0).start()
            f_copy(p, 1).start()
        for p in range(2):
            f_copy(p, 0).wait_recv()
            f_copy(p, 2).start()
        for p in range(2):
            f_copy(p, 1).wait_recv()
            f_copy(p, 2).wait_recv()
        for p in range(2):
            for k in range(3):
                f_copy(p, k).wait_send()

    leader = (d == 2) & last_phase

    @pl.when(jnp.logical_not(leader))
    def _():
        sr_copy(1).wait_recv()

    stat_ref[...] = sres[...]

    @pl.when(leader)
    def _():
        for k in range(1, 4):
            st_copy(k).wait_send()
        for k in range(1, 8):
            sr_copy(k).wait_send()

    for t in range(2):

        @pl.when(hops & (d != t))
        def _():
            kv_hop(t).wait_send()

            @pl.when(last_phase)
            def _():
                row_send(t).wait_send()

    @pl.when(first_phase)
    def _():
        hx_copy().wait_send()

        @pl.when(d < 2)
        def _():
            for p in range(2):
                adj_send(p).wait_send()
                pair_copy(p).wait_send()
                for b in (2, 3):
                    for k in range(3):
                        spread(b, p, k).wait_send()
            for g in range(8):
                q_copy(g).wait_send()
                m_copy(g).wait_send()

        @pl.when(d >= 2)
        def _():
            kv_x().wait_send()
            for p in range(2):
                far_zero(p).wait_send()
                far_send(p).wait_send()
            for g in range(8):
                o_copy(g).wait_send()
                y_copy(g).wait_send()

                @pl.when(d != keeper(g))
                def _():
                    z_copy(g).wait_send()

                @pl.when(d == keeper(g))
                def _():
                    u_copy(g).wait_send()

    @pl.when(last_phase)
    def _():
        @pl.when(d != 2)
        def _():
            hr_send().wait_send()

        @pl.when(d < 2)
        def _():
            w_query().wait_send()
            m_copy(0).wait_send()

        @pl.when(d == 3)
        def _():
            w_out().wait_send()

        @pl.when(d == 2)
        def _():
            for k in range(1, 4):
                p_copy(k).wait_send()

        @pl.when(d >= 2)
        def _():
            for p in range(2):
                kv_relay(p).wait_send()


def kept_shards(hidden, norm_gain, kv_weight, attn_flat, final_gain, reward_head, segment_ids, ranks):
    width = hidden.shape[2]
    responses = ranks.shape[0]
    vmem = pl.BlockSpec(memory_space=pltpu.VMEM)
    anywhere = pl.BlockSpec(memory_space=pl.ANY)
    dma = pltpu.SemaphoreType.DMA
    V = pltpu.VMEM
    moved, stats = pl.pallas_call(
        relay_kernel,
        out_shape=(
            jax.ShapeDtypeStruct((128, 4096), BF),
            jax.ShapeDtypeStruct((responses, 8, 128), F32),
        ),
        in_specs=[
            vmem,
            vmem,
            anywhere,
            anywhere,
            pl.BlockSpec(memory_space=pltpu.SMEM),
            vmem,
            vmem,
        ],
        out_specs=(vmem, vmem),
        scratch_shapes=[
            V((4096, 512), BF),
            V((1, 1, 2097152), BF),
            V((2048, 1024), BF),
            V((512, 4096), BF),
            V((128, 4096), BF),
            V((4, 128, 2048), BF),
            V((2, 128, 256), BF),
            V((4, 128, 256), BF),
            V((8, 64, 512), BF),
            V((8, 64, 512), F32),
            V((8, 64, 512), BF),
            V((8, 64, 512), BF),
            V((8, 64, 512), BF),
            V((8, 64, 2048), BF),
            V((8, 64, 2048), F32),
            V((8, 64, 2048), BF),
            V((8, 64, 1024), BF),
            V((8, 64, 1024), F32),
            V((8, 64, 1024), BF),
            V((8, 64, 1024), BF),
            V((8, 64, 1024), BF),
            V((8, 64, 1024), BF),
            V((2, 64, 1024), BF),
            V((128, 1024), BF),
            V((64, 1024), BF),
            V((2, 16, 2048), BF),
            V((2, 128, 256), BF),
            V((64, 512), F32),
            V((64, 512), F32),
            V((8, 4096), F32),
            V((8, 4096), F32),
            V((4, 8, 1024), F32),
            V((4, 8, 1024), F32),
            V((4, responses, 8, 128), F32),
            V((responses, 8, 128), F32),
            dma((5,)),
            dma((2,)),
            dma((2,)),
            dma((2,)),
            dma((2,)),
            dma((2,)),
            dma((2, 2)),
            dma((2, 2, 3)),
            dma((2, 2, 3)),
            dma((2,)),
            dma((4,)),
            dma((2,)),
            dma((4,)),
            dma(()),
            dma(()),
            dma(()),
            dma((4,)),
            dma((2,)),
            dma((2,)),
            dma((2,)),
            dma(()),
            dma(()),
            dma((2,)),
            dma((2,)),
            dma((2,)),
            dma((3,)),
            dma((3,)),
            dma((8,)),
            dma((8,)),
            dma((8,)),
            dma((8,)),
            dma((8,)),
            dma((8,)),
            dma((8,)),
            dma((8,)),
            dma((8,)),
            dma((8,)),
            dma((8,)),
            dma((2,)),
            dma((2, 3)),
            dma((2, 3)),
            dma((3,)),
            dma((3,)),
            dma((7,)),
            dma(()),
        ],
        compiler_params=pltpu.CompilerParams(
            collective_id=0, has_side_effects=True, vmem_limit_bytes=60 << 20
        ),
    )(
        hidden[0],
        norm_gain,
        kv_weight,
        attn_flat,
        segment_ids,
        final_gain[None],
        reward_head[None],
    )
    rewards = stats[:, 4, 0] * lax.rsqrt(stats[:, 0, 0] / width + EPS)
    pair_loss = jnp.where(
        ranks[:, None] < ranks[None, :], jax.nn.softplus(rewards[None, :] - rewards[:, None]), 0.0
    )
    return (moved[None], rewards, pair_loss)


def shards(hidden, norm_gain, kv_weight, attn_flat, final_gain, reward_head, segment_ids, ranks):
    blocks = lax.axis_size("dp")
    lanes = lax.axis_size("mp")
    kv_local = kv_weight.shape[2] // (2 * HD)
    kept = (
        (lax.axis_size("section"), blocks, lanes, kv_local) == (2, 4, 4, 2)
        and hidden.shape[1:] == (128, 4096)
        and attn_flat.shape == (1, 1, 2097152)
    )
    args = (hidden, norm_gain, kv_weight, attn_flat, final_gain, reward_head, segment_ids, ranks)
    return (kept_shards if kept else gathered_shards)(*args)


def solution(mesh):
    placed = (
        P("section", "dp", None),
        P("section", None),
        P("section", None, "mp"),
        P("section", "mp", "dp"),
        P(),
        P(),
        P("section", None),
        P(),
    )
    return jax.shard_map(
        shards,
        mesh=mesh,
        in_specs=placed,
        out_specs=(P("section", "dp", None), P(), P()),
        check_vma=False,
    )
```

```python
import functools

import jax
import jax.numpy as jnp
from jax import lax
from jax.experimental import pallas as pl
from jax.experimental.pallas import tpu as pltpu
from jax.sharding import PartitionSpec as P

HD = 128
QH = 32
KVH = 8


EPS = 1e-05


def passed_along(block, axis, distance):
    devices = range(lax.axis_size(axis))
    route = [(i - distance, i) for i in devices if i - distance in devices]
    return lax.ppermute(block, axis, route)


def gathered_shards(hidden, norm_gain, kv_weight, attn_flat, final_gain, reward_head, segment_ids, ranks):
    state = hidden[0]
    tokens = state.shape[0]
    width = state.shape[1]
    seg_row = segment_ids[0]
    blocks = lax.axis_size("dp")
    block = lax.axis_index("dp")
    phases = lax.axis_size("section")
    phase_now = lax.axis_index("section")
    responses = ranks.shape[0]
    state_wide = state.astype(jnp.float32)
    normed = (
        state_wide
        * lax.rsqrt(jnp.mean(state_wide * state_wide, -1, keepdims=True) + EPS)
        * norm_gain[0]
    ).astype(jnp.bfloat16)
    keyval = jnp.dot(normed, kv_weight[0], preferred_element_type=jnp.float32).astype(jnp.bfloat16)
    kv_local = keyval.shape[1] // (2 * HD)
    group = QH // KVH
    q_width = kv_local * group * HD
    flat = lax.all_gather(attn_flat[0, 0], "dp", axis=0, tiled=True)
    w_query = flat[: width * q_width].reshape(width, q_width)
    w_out = flat[width * q_width : 2 * width * q_width].reshape(q_width, width)
    query = jnp.dot(normed, w_query, preferred_element_type=jnp.float32).astype(jnp.bfloat16)
    query = query.reshape(tokens, kv_local, group, HD)
    block_ids = jnp.arange(blocks, dtype=jnp.int32)
    own_seg = jnp.sum(jnp.where(block_ids == block, seg_row, 0))
    query_pos = block * tokens + jnp.arange(tokens, dtype=jnp.int32)
    piece = lax.all_gather(keyval, "dp", axis=0, tiled=True)
    peak = jnp.full((kv_local, group, tokens), -1e30, jnp.float32)
    count = piece.shape[0]
    key_pos = jnp.arange(count, dtype=jnp.int32)
    key_block = key_pos // tokens
    key_seg = jnp.sum(jnp.where(key_block[:, None] == block_ids[None, :], seg_row[None, :], 0), 1)
    parts = piece.reshape(count, kv_local, 2, HD)
    keys = parts[:, :, 0]
    values = parts[:, :, 1]
    earlier = (key_block < block) & (key_block >= 0) & ((key_seg == 0) | (key_seg == own_seg))
    same = (key_block == block)[None, :] & (key_pos[None, :] <= query_pos[:, None])
    visible = earlier[None, :] | same
    scores = jnp.einsum("tjgd,cjd->jgtc", query, keys, preferred_element_type=jnp.float32) * HD ** (
        -0.5
    )
    scores = jnp.where(visible[None, None], scores, -1e30)
    new_peak = jnp.maximum(peak, jnp.max(scores, -1))
    weights = jnp.where(visible[None, None], jnp.exp(scores - new_peak[..., None]), 0.0)
    total = jnp.sum(weights, -1)
    accum = jnp.einsum(
        "jgtc,cjd->jgtd", weights.astype(jnp.bfloat16), values, preferred_element_type=jnp.float32
    )
    peak, total, accum = (new_peak, total, accum)
    mixed = (
        (accum / total[..., None])
        .transpose(2, 0, 1, 3)
        .reshape(tokens, q_width)
        .astype(jnp.bfloat16)
    )
    partial_value = jnp.dot(mixed, w_out, preferred_element_type=jnp.float32)
    ends = (
        jnp.sum(
            (seg_row[None, :] <= jnp.arange(1, responses + 1, dtype=jnp.int32)[:, None]).astype(
                jnp.int32
            ),
            1,
        )
        - 1
    )
    at_end = (ends == block) & (phase_now == phases - 1)
    summed = lax.psum(partial_value.astype(jnp.bfloat16), "mp").astype(jnp.float32)
    updated = (state_wide + summed).astype(jnp.bfloat16)
    moved = passed_along(updated, "section", 1)
    last_row = updated[tokens - 1].astype(jnp.float32)
    squares = jnp.sum(last_row * last_row)
    product = jnp.sum(last_row * final_gain * reward_head)
    sums_sq, dots = lax.psum(
        (jnp.where(at_end, squares, 0.0), jnp.where(at_end, product, 0.0)), ("section", "dp")
    )
    rewards = dots * lax.rsqrt(sums_sq / width + EPS)
    pair_loss = jnp.where(
        ranks[:, None] < ranks[None, :], jax.nn.softplus(rewards[None, :] - rewards[:, None]), 0.0
    )
    return (moved[None], rewards, pair_loss)


BF = jnp.bfloat16
F32 = jnp.float32
HIDE = -1e30


def copy_to(src, dst, send, recv, **where):
    return pltpu.make_async_remote_copy(
        src_ref=src,
        dst_ref=dst,
        send_sem=send,
        recv_sem=recv,
        device_id=where,
        device_id_type=pl.DeviceIdType.MESH,
    )


def relay_kernel(
    h_ref,
    gain_ref,
    kvw_hbm,
    flat_hbm,
    seg_ref,
    fg_ref,
    rh_ref,
    out_ref,
    stat_ref,
    kvw,
    flat,
    wq,
    wo,
    nrm,
    xq,
    kvs,
    kvr,
    qs,
    qo,
    qr,
    mx,
    mr,
    osend,
    oown,
    orecv,
    ysend,
    yown,
    yrecv,
    zsend,
    zrecv,
    us,
    uin,
    hx,
    hrow,
    rx,
    rkv,
    qs1,
    qr1,
    osum,
    zin,
    psum,
    pin,
    st,
    sres,
    load_sem,
    adj_s,
    adj_r,
    pair_s,
    pair_r,
    far_s,
    far_r,
    sp_s,
    sp_r,
    row_s,
    row_r,
    kv_s,
    kv_r,
    hx_s,
    hx_r,
    hr_s,
    hr_r,
    rx_s,
    rx_r,
    rl_s,
    kx_s,
    kx_r,
    rk_s,
    w_s,
    w_r,
    p_s,
    p_r,
    q_s,
    q_r,
    m_s,
    m_r,
    o_s,
    o_r,
    y_s,
    y_r,
    z_s,
    z_r,
    u_s,
    u_r,
    f_s,
    f_r,
    st_s,
    st_r,
    sr_s,
    sr_r,
):
    s = lax.axis_index("section")
    d = lax.axis_index("dp")
    m = lax.axis_index("mp")
    y = m // 2
    c = m % 2
    across = (m + 2) % 4
    beside = m + 1 - 2 * c
    first_phase = s == 0
    last_phase = s == 1
    load_kv = pltpu.make_async_copy(kvw_hbm.at[0], kvw, load_sem.at[0])
    CH = 4
    SPAN = 2097152 // CH

    def load_flat(i):
        cut = slice(i * SPAN, (i + 1) * SPAN)
        return pltpu.make_async_copy(
            flat_hbm.at[:, :, cut], flat.at[:, :, cut], load_sem.at[1 + i]
        )

    @pl.when(d >= 2)
    def _():
        load_kv.start()

    for i in range(CH):
        load_flat(i).start()

    @pl.when(d < 2)
    def _():
        load_kv.start()

    barrier = pltpu.get_barrier_semaphore()
    for k in range(1, 4):
        pl.semaphore_signal(
            barrier, inc=1, device_id={"mp": (m + k) % 4}, device_id_type=pl.DeviceIdType.MESH
        )
    for k in range(1, 8):
        t = (s * 4 + d + k) % 8
        pl.semaphore_signal(
            barrier,
            inc=1,
            device_id={"section": t // 4, "dp": t % 4},
            device_id_type=pl.DeviceIdType.MESH,
        )
    h = h_ref[...].astype(F32)
    scale = lax.rsqrt(jnp.mean(h * h, -1, keepdims=True) + EPS)
    nrm[...] = (h * scale * gain_ref[...]).astype(BF)

    mine_out = pl.ds(pl.multiple_of((2 * c + y) * 1024, 1024), 1024)
    across_out = pl.ds(pl.multiple_of((2 * c + 1 - y) * 1024, 1024), 1024)

    natural = pl.ds(pl.multiple_of(m * 1024, 1024), 1024)

    def halves(t):
        return slice(t * 2048, (t + 1) * 2048)

    def keyval():
        load_kv.wait()
        for t in range(2):
            kvs[t] = jnp.dot(
                nrm[...], kvw[:, t * 256 : (t + 1) * 256], preferred_element_type=F32
            ).astype(BF)

            @pl.when(d == t)
            def _():
                kvr[t] = kvs[t]

    def shape_query():
        for i in range(CH):
            load_flat(i).wait()

            @pl.loop(0, 32 // CH)
            def _(k):
                k = k + i * (32 // CH)
                part = flat[0, :, pl.ds(pl.multiple_of(k * 65536, 65536), 65536)].astype(F32)
                wq[pl.ds(pl.multiple_of(k * 64, 64), 64), :] = part.reshape(64, 1024).astype(BF)

    def shape_out():
        for i in range(CH):
            load_flat(i).wait()

            @pl.loop(0, 32 // CH)
            def _(k):
                k = k + i * (32 // CH)
                part = flat[0, :, pl.ds(pl.multiple_of(k * 65536, 65536), 65536)].astype(F32)
                wo[pl.ds(pl.multiple_of(k * 16, 16), 16), :] = part.reshape(16, 4096).astype(BF)

    @pl.when(first_phase)
    def _():
        for t in range(2):

            @pl.when(d == t)
            def _():
                xq[t] = nrm[:, halves(t)]

    @pl.when(last_phase)
    def _():
        for b in range(4):
            for t in range(2):
                if b == t:

                    @pl.when(d == b)
                    def _():
                        xq[0, 16 * b : 16 * b + 16] = nrm[112:128, halves(t)]

    @pl.when(d < 2)
    def _():
        shape_query()

    pl.semaphore_wait(barrier, 10)

    def pair_rows(p):
        return pl.ds(pl.multiple_of(p * 64 + c * 32, 32), 32)

    def adj_send(p):
        rows = pair_rows(p)
        cols = pl.ds(pl.multiple_of((1 - d) * 2048, 2048), 2048)
        return copy_to(
            nrm.at[rows, cols], xq.at[d, rows], adj_s.at[p], adj_r.at[p], dp=1 - d
        )

    def adj_arrive(p):
        rows = pair_rows(p)
        return copy_to(
            xq.at[1 - d, rows], xq.at[1 - d, rows], adj_s.at[p], adj_r.at[p], dp=1 - d
        )

    def pair_copy(p):
        rows = pair_rows(p)
        return copy_to(
            xq.at[1 - d, rows], xq.at[1 - d, rows], pair_s.at[p], pair_r.at[p], mp=beside
        )

    def quarter(p, which):
        return pl.ds(pl.multiple_of(p * 64 + which * 16, 16), 16)

    def far_send(p):
        rows = quarter(p, m)
        return copy_to(
            nrm.at[rows, halves(1)], xq.at[d, rows], far_s.at[p], far_r.at[d - 2, p], dp=1
        )

    def far_zero(p):
        rows = quarter(p, m)
        return copy_to(
            nrm.at[rows, halves(0)], xq.at[d, rows], rx_s.at[p], far_r.at[d - 2, p], dp=0
        )

    def x_hop(p):
        return copy_to(
            nrm.at[quarter(p, m), halves(0)], rx.at[p], rx_s.at[p], rx_r.at[p], section=1
        )

    def x_relay(p):
        return pltpu.make_async_remote_copy(
            src_ref=rx.at[p],
            dst_ref=xq.at[d, quarter(p, m)],
            send_sem=rl_s.at[p],
            recv_sem=far_r.at[d - 2, p],
            device_id={"section": 0, "dp": 0},
            device_id_type=pl.DeviceIdType.MESH,
        )

    def kv_x():
        return copy_to(kvs, rkv, kx_s, kx_r, section=1)

    def kv_relay(t):
        return pltpu.make_async_remote_copy(
            src_ref=rkv.at[t],
            dst_ref=kvr.at[d],
            send_sem=rk_s.at[t],
            recv_sem=kv_r.at[d],
            device_id={"section": 0, "dp": t},
            device_id_type=pl.DeviceIdType.MESH,
        )

    def far_arrive(b, p):
        rows = quarter(p, m)
        return copy_to(
            xq.at[b, rows], xq.at[b, rows], far_s.at[p], far_r.at[b - 2, p], dp=b
        )

    def spread(b, p, k):
        rows = quarter(p, across if k == 2 else m)
        return copy_to(
            xq.at[b, rows],
            xq.at[b, rows],
            sp_s.at[b - 2, p, k],
            sp_r.at[b - 2, p, k],
            mp=across if k == 0 else beside,
        )

    def row_send(t):
        return copy_to(
            nrm.at[112:128, halves(t)],
            xq.at[0, pl.ds(pl.multiple_of(d * 16, 16), 16)],
            row_s.at[t],
            row_r.at[d],
            dp=t,
        )

    def row_arrive(b):
        rows = slice(16 * b, 16 * b + 16)
        return copy_to(xq.at[0, rows], xq.at[0, rows], row_s.at[0], row_r.at[b], dp=b)

    def kv_hop(t):
        return copy_to(kvs.at[t], kvr.at[d], kv_s.at[t], kv_r.at[d], dp=t)

    def kv_arrive(b):
        return copy_to(kvr.at[b], kvr.at[b], kv_s.at[0], kv_r.at[b], dp=b)

    def hx_copy():
        return copy_to(h_ref.at[:, mine_out], hx, hx_s, hx_r, section=1 - s)

    def hr_send():
        return copy_to(
            h_ref.at[112:128, natural],
            hrow.at[pl.ds(pl.multiple_of(d * 16, 16), 16)],
            hr_s,
            hr_r.at[d],
            dp=2,
        )

    def hr_arrive(b):
        rows = slice(16 * b, 16 * b + 16)
        return copy_to(hrow.at[rows], hrow.at[rows], hr_s, hr_r.at[b], dp=b)

    @pl.when(first_phase)
    def _():
        @pl.when(d < 2)
        def _():
            for p in range(2):
                adj_send(p).start()

        @pl.when(d == 2)
        def _():
            for p in range(2):
                far_send(p).start()
                far_zero(p).start()

    @pl.when(last_phase)
    def _():
        for t in range(2):

            @pl.when(d != t)
            def _():
                row_send(t).start()

    keyval()
    hops = (d < 2) | last_phase
    for t in range(2):

        @pl.when(hops & (d != t))
        def _():
            kv_hop(t).start()

    @pl.when((d >= 2) & first_phase)
    def _():
        kv_x().start()

        @pl.when(d == 3)
        def _():
            for p in range(2):
                far_send(p).start()
                far_zero(p).start()

    @pl.when(first_phase)
    def _():
        @pl.when(d < 2)
        def _():
            hx_copy().start()

        out_ref[...] = jnp.zeros_like(out_ref)

    @pl.when(last_phase)
    def _():
        @pl.when(d != 2)
        def _():
            hr_send().start()

        @pl.when(d == 2)
        def _():
            hrow[32:48] = h_ref[112:128, natural]

    def q_copy(g):
        return copy_to(qs.at[g], qr.at[g], q_s.at[g], q_r.at[g], dp=1 - d)

    def m_copy(g):
        return copy_to(mx.at[g], mr.at[g], m_s.at[g], m_r.at[g], dp=d + 2)

    def m_arrive(g):
        return copy_to(mr.at[g], mr.at[g], m_s.at[g], m_r.at[g], dp=d - 2)

    def w_query():
        return copy_to(qs1, qr1, w_s.at[0], w_r.at[0], dp=1 - d)

    def w_out():
        return copy_to(osum, zin, w_s.at[1], w_r.at[1], dp=5 - d)

    def project(g):
        b, rows = g // 2, slice(g % 2 * 64, g % 2 * 64 + 64)
        mine = pl.ds(pl.multiple_of(d * 512, 512), 512)
        other = pl.ds(pl.multiple_of((1 - d) * 512, 512), 512)
        qs[g] = jnp.dot(xq[b, rows], wq[:, other], preferred_element_type=F32).astype(BF)
        q_copy(g).start()
        qo[g] = jnp.dot(xq[b, rows], wq[:, mine], preferred_element_type=F32)

    def attend(g, blocks, mask):
        q_copy(g).wait_recv()
        mix(g, qo[g] + qr[g].astype(F32), blocks, mask)

        m_copy(g).start()

    def mix(g, q, blocks, mask):
        q = q.astype(BF)
        q = jnp.concatenate([q[:, j * HD : (j + 1) * HD] for j in range(4)], 0)
        scores = []
        for j in range(blocks):
            score = (
                lax.dot_general(
                    q, kvr[j, :, :HD], (((1,), (1,)), ((), ())), preferred_element_type=F32
                )
                * HD ** (-0.5)
            )
            scores.append(mask(j, score))
        peak = functools.reduce(jnp.maximum, [jnp.max(x, -1, keepdims=True) for x in scores])
        total = jnp.zeros_like(peak)
        mixed = jnp.zeros((256, HD), F32)
        for j in range(blocks):
            weight = jnp.exp(scores[j] - peak)
            total = total + jnp.sum(weight, -1, keepdims=True)
            mixed = mixed + jnp.dot(
                weight.astype(BF), kvr[j, :, HD:], preferred_element_type=F32
            )
        mixed = (mixed / total).astype(BF)
        for j in range(4):
            mx[g, :, j * HD : (j + 1) * HD] = mixed[j * 64 : (j + 1) * 64]

    def block_mask(g):
        b, half = g // 2, g % 2

        def mask(j, score):
            if j < b:
                seen = (seg_ref[0, j] == 0) | (seg_ref[0, j] == seg_ref[0, b])
                return score + jnp.where(seen, 0.0, HIDE)
            row = lax.broadcasted_iota(jnp.int32, score.shape, 0) % 64 + half * 64
            col = lax.broadcasted_iota(jnp.int32, score.shape, 1)
            return jnp.where(col <= row, score, HIDE)

        return mask

    def ends_mask(j, score):
        row = lax.broadcasted_iota(jnp.int32, score.shape, 0) % 64
        col = lax.broadcasted_iota(jnp.int32, score.shape, 1)
        of = row // 16
        own = jnp.zeros_like(row)
        for b in range(4):
            own = own + jnp.where(of == b, seg_ref[0, b], 0)
        earlier = (of > j) & ((own == seg_ref[0, j]) | (seg_ref[0, j] == 0))
        same = (of == j) & (col <= row % 16 + 112)
        return jnp.where(earlier | same, score, HIDE)

    @pl.when((d < 2) & first_phase)
    def _():
        def adjacent(p):
            adj_arrive(p).wait_recv()
            pair_copy(p).start()

        def joined(p):
            pair_copy(p).wait_recv()

        def receive(b, p):
            far_arrive(b, p).wait_recv()
            spread(b, p, 0).start()
            spread(b, p, 1).start()

        def forward(b, p):
            spread(b, p, 0).wait_recv()
            spread(b, p, 2).start()

        def complete(b, p):
            spread(b, p, 1).wait_recv()
            spread(b, p, 2).wait_recv()

        def keys(b):
            @pl.when(d != b)
            def _():
                kv_arrive(b).wait_recv()

        def paired(g):
            @pl.when(d != g // 2)
            def _():
                joined(g % 2)

        adjacent(0)
        paired(0)
        project(0)
        adjacent(1)
        paired(1)
        project(1)
        keys(0)
        attend(0, 1, block_mask(0))
        paired(2)
        project(2)
        receive(2, 0)
        attend(1, 1, block_mask(1))
        receive(2, 1)
        paired(3)
        project(3)
        keys(1)
        forward(2, 0)
        attend(2, 2, block_mask(2))
        forward(2, 1)
        complete(2, 0)
        project(4)
        receive(3, 0)
        attend(3, 2, block_mask(3))
        receive(3, 1)
        complete(2, 1)
        project(5)
        forward(3, 0)
        keys(2)
        attend(4, 3, block_mask(4))
        forward(3, 1)
        complete(3, 0)
        project(6)
        attend(5, 3, block_mask(5))
        complete(3, 1)
        project(7)
        keys(3)
        attend(6, 4, block_mask(6))
        attend(7, 4, block_mask(7))

    @pl.when((d < 2) & last_phase)
    def _():
        for b in range(4):

            @pl.when(d != b)
            def _():
                row_arrive(b).wait_recv()

        mine = pl.ds(pl.multiple_of(d * 512, 512), 512)
        other = pl.ds(pl.multiple_of((1 - d) * 512, 512), 512)
        qs1[...] = jnp.dot(xq[0, 0:64], wq[:, other], preferred_element_type=F32)
        w_query().start()
        own = jnp.dot(xq[0, 0:64], wq[:, mine], preferred_element_type=F32)
        for b in range(4):

            @pl.when(d != b)
            def _():
                kv_arrive(b).wait_recv()

        w_query().wait_recv()
        mix(0, own + qr1[...], 4, ends_mask)
        m_copy(0).start()

    def o_copy(g):
        return copy_to(osend.at[g], orecv.at[g], o_s.at[g], o_r.at[g], mp=beside)

    def y_copy(g):
        return copy_to(ysend.at[g], yrecv.at[g], y_s.at[g], y_r.at[g], mp=across)

    def z_copy(g):
        return copy_to(zsend.at[g], zrecv.at[g], z_s.at[g], z_r.at[g], dp=5 - d)

    def u_copy(g):
        return pltpu.make_async_remote_copy(
            src_ref=us.at[g],
            dst_ref=uin.at[g % 2],
            send_sem=u_s.at[g],
            recv_sem=u_r.at[g % 2],
            device_id={"section": 1, "dp": g // 2},
            device_id_type=pl.DeviceIdType.MESH,
        )

    def keeper(g):
        return 3 if g >= 6 else 2

    def first(g):
        m_arrive(g).wait_recv()
        mine = pl.ds(pl.multiple_of(c * 2048, 2048), 2048)
        other = pl.ds(pl.multiple_of((1 - c) * 2048, 2048), 2048)
        osend[g] = jnp.dot(mr[g], wo[:, other], preferred_element_type=F32).astype(BF)
        o_copy(g).start()
        oown[g] = jnp.dot(mr[g], wo[:, mine], preferred_element_type=F32)

    def second(g):
        o_copy(g).wait_recv()
        mine = pl.ds(pl.multiple_of(y * 1024, 1024), 1024)
        other = pl.ds(pl.multiple_of((1 - y) * 1024, 1024), 1024)
        ysend[g] = (oown[g, :, other] + orecv[g, :, other].astype(F32)).astype(BF)
        y_copy(g).start()
        yown[g] = oown[g, :, mine] + orecv[g, :, mine].astype(F32)

    def third(g):
        y_copy(g).wait_recv()

        @pl.when(d != keeper(g))
        def _():
            zsend[g] = (yown[g] + yrecv[g].astype(F32)).astype(BF)
            z_copy(g).start()

        @pl.when(d == keeper(g))
        def _():
            yown[g] = yown[g] + yrecv[g].astype(F32)

    def fourth(g):
        @pl.when(d == keeper(g))
        def _():
            z_copy(g).wait_recv()
            us[g] = (yown[g] + zrecv[g].astype(F32)).astype(BF)
            u_copy(g).start()

    @pl.when((d >= 2) & last_phase)
    def _():
        copy_to(rkv, rkv, kx_s, kx_r, section=0).wait_recv()
        for t in (1, 0):
            kv_relay(t).start()

    @pl.when(d >= 2)
    def _():
        shape_out()

        @pl.when(first_phase)
        def _():
            hx_copy().start()

    @pl.when((d >= 2) & first_phase)
    def _():
        for g in range(12):
            if g < 8:
                first(g)
            if 0 <= g - 2 < 8:
                third(g - 2)
            if 0 <= g - 4 < 8:
                fourth(g - 4)
            if g < 8:
                second(g)

    def st_copy(k):
        t = (m + k) % 4
        return copy_to(st.at[m], st.at[m], st_s.at[k - 1], st_r.at[k - 1], mp=t)

    def st_arrive(k):
        t = (m + 4 - k) % 4
        return copy_to(st.at[t], st.at[t], st_s.at[k - 1], st_r.at[k - 1], mp=t)

    def sr_copy(k):
        t = (6 + k) % 8
        return pltpu.make_async_remote_copy(
            src_ref=sres,
            dst_ref=sres,
            send_sem=sr_s.at[k - 1],
            recv_sem=sr_r,
            device_id={"section": t // 4, "dp": t % 4},
            device_id_type=pl.DeviceIdType.MESH,
        )

    def p_copy(k):
        t = (m + k) % 4
        return copy_to(psum.at[t], pin.at[m], p_s.at[k - 1], p_r.at[k - 1], mp=t)

    def p_arrive(k):
        t = (m + 4 - k) % 4
        return copy_to(pin.at[t], pin.at[t], p_s.at[k - 1], p_r.at[k - 1], mp=t)

    def last_rows(a):
        rest = jnp.zeros((4, a.shape[1]), F32)
        return jnp.concatenate([a[16 * b + 15 : 16 * b + 16] for b in range(4)] + [rest], 0)

    @pl.when((d >= 2) & last_phase)
    def _():
        m_arrive(0).wait_recv()
        for k in range(4):
            cols = slice(k * 1024, k * 1024 + 1024)
            osum[:, cols] = last_rows(jnp.dot(mr[0], wo[:, cols], preferred_element_type=F32))

        @pl.when(d == 3)
        def _():
            w_out().start()

    @pl.when((d == 2) & last_phase)
    def _():
        for b in (0, 1, 3):
            hr_arrive(b).wait_recv()
        w_out().wait_recv()
        for k in range(4):
            cols = slice(k * 1024, k * 1024 + 1024)
            psum[k] = (osum[:, cols] + zin[:, cols]).astype(BF).astype(F32)
        pin[m] = psum[m]
        for k in range(1, 4):
            p_copy(k).start()
        for k in range(1, 4):
            p_arrive(k).wait_recv()
        total = (pin[0] + pin[1]) + (pin[2] + pin[3])
        v = (last_rows(hrow[...].astype(F32)) + total).astype(BF).astype(F32)
        squares = jnp.sum(v * v, -1, keepdims=True)
        product = jnp.sum(v * fg_ref[:, natural] * rh_ref[:, natural], -1, keepdims=True)
        spot = lax.broadcasted_iota(jnp.int32, squares.shape, 0)
        half = lax.broadcasted_iota(jnp.int32, (8, 128), 0) < 4
        for r in range(sres.shape[0]):
            end = -1
            for b in range(4):
                end = end + jnp.where(seg_ref[0, b] <= r + 1, 1, 0)
            here = spot == end
            one = jnp.sum(jnp.where(here, squares, 0.0), keepdims=True)
            two = jnp.sum(jnp.where(here, product, 0.0), keepdims=True)
            st[m, r] = jnp.where(half, one, two)
        for k in range(1, 4):
            st_copy(k).start()
        for k in range(1, 4):
            st_arrive(k).wait_recv()
        sres[...] = (st[0] + st[1]) + (st[2] + st[3])
        for k in range(1, 8):
            sr_copy(k).start()

    @pl.when(last_phase)
    def _():
        def f_copy(p, k):
            rows = slice(p * 64, p * 64 + 64)
            cols = across_out if k == 2 else mine_out
            return copy_to(
                out_ref.at[rows, cols],
                out_ref.at[rows, cols],
                f_s.at[p, k],
                f_r.at[p, k],
                mp=across if k == 0 else beside,
            )

        def u_arrive(p):
            return copy_to(uin.at[p], uin.at[p], u_s.at[p], u_r.at[p], section=0)

        copy_to(hx, hx, hx_s, hx_r, section=0).wait_recv()
        for p in range(2):
            rows = slice(p * 64, p * 64 + 64)
            u_arrive(p).wait_recv()
            out_ref[rows, mine_out] = (
                hx[rows].astype(F32) + uin[p].astype(F32)
            ).astype(BF)
            f_copy(p, 0).start()
            f_copy(p, 1).start()
        for p in range(2):
            f_copy(p, 0).wait_recv()
            f_copy(p, 2).start()
        for p in range(2):
            f_copy(p, 1).wait_recv()
            f_copy(p, 2).wait_recv()
        for p in range(2):
            for k in range(3):
                f_copy(p, k).wait_send()

    leader = (d == 2) & last_phase

    @pl.when(jnp.logical_not(leader))
    def _():
        sr_copy(1).wait_recv()

    stat_ref[...] = sres[...]

    @pl.when(leader)
    def _():
        for k in range(1, 4):
            st_copy(k).wait_send()
        for k in range(1, 8):
            sr_copy(k).wait_send()

    for t in range(2):

        @pl.when(hops & (d != t))
        def _():
            kv_hop(t).wait_send()

            @pl.when(last_phase)
            def _():
                row_send(t).wait_send()

    @pl.when(first_phase)
    def _():
        hx_copy().wait_send()

        @pl.when(d < 2)
        def _():
            for p in range(2):
                adj_send(p).wait_send()
                pair_copy(p).wait_send()
                for b in (2, 3):
                    for k in range(3):
                        spread(b, p, k).wait_send()
            for g in range(8):
                q_copy(g).wait_send()
                m_copy(g).wait_send()

        @pl.when(d >= 2)
        def _():
            kv_x().wait_send()
            for p in range(2):
                far_zero(p).wait_send()
                far_send(p).wait_send()
            for g in range(8):
                o_copy(g).wait_send()
                y_copy(g).wait_send()

                @pl.when(d != keeper(g))
                def _():
                    z_copy(g).wait_send()

                @pl.when(d == keeper(g))
                def _():
                    u_copy(g).wait_send()

    @pl.when(last_phase)
    def _():
        @pl.when(d != 2)
        def _():
            hr_send().wait_send()

        @pl.when(d < 2)
        def _():
            w_query().wait_send()
            m_copy(0).wait_send()

        @pl.when(d == 3)
        def _():
            w_out().wait_send()

        @pl.when(d == 2)
        def _():
            for k in range(1, 4):
                p_copy(k).wait_send()

        @pl.when(d >= 2)
        def _():
            for p in range(2):
                kv_relay(p).wait_send()


def kept_shards(hidden, norm_gain, kv_weight, attn_flat, final_gain, reward_head, segment_ids, ranks):
    width = hidden.shape[2]
    responses = ranks.shape[0]
    vmem = pl.BlockSpec(memory_space=pltpu.VMEM)
    anywhere = pl.BlockSpec(memory_space=pl.ANY)
    dma = pltpu.SemaphoreType.DMA
    V = pltpu.VMEM
    moved, stats = pl.pallas_call(
        relay_kernel,
        out_shape=(
            jax.ShapeDtypeStruct((128, 4096), BF),
            jax.ShapeDtypeStruct((responses, 8, 128), F32),
        ),
        in_specs=[
            vmem,
            vmem,
            anywhere,
            anywhere,
            pl.BlockSpec(memory_space=pltpu.SMEM),
            vmem,
            vmem,
        ],
        out_specs=(vmem, vmem),
        scratch_shapes=[
            V((4096, 512), BF),
            V((1, 1, 2097152), BF),
            V((2048, 1024), BF),
            V((512, 4096), BF),
            V((128, 4096), BF),
            V((4, 128, 2048), BF),
            V((2, 128, 256), BF),
            V((4, 128, 256), BF),
            V((8, 64, 512), BF),
            V((8, 64, 512), F32),
            V((8, 64, 512), BF),
            V((8, 64, 512), BF),
            V((8, 64, 512), BF),
            V((8, 64, 2048), BF),
            V((8, 64, 2048), F32),
            V((8, 64, 2048), BF),
            V((8, 64, 1024), BF),
            V((8, 64, 1024), F32),
            V((8, 64, 1024), BF),
            V((8, 64, 1024), BF),
            V((8, 64, 1024), BF),
            V((8, 64, 1024), BF),
            V((2, 64, 1024), BF),
            V((128, 1024), BF),
            V((64, 1024), BF),
            V((2, 16, 2048), BF),
            V((2, 128, 256), BF),
            V((64, 512), F32),
            V((64, 512), F32),
            V((8, 4096), F32),
            V((8, 4096), F32),
            V((4, 8, 1024), F32),
            V((4, 8, 1024), F32),
            V((4, responses, 8, 128), F32),
            V((responses, 8, 128), F32),
            dma((5,)),
            dma((2,)),
            dma((2,)),
            dma((2,)),
            dma((2,)),
            dma((2,)),
            dma((2, 2)),
            dma((2, 2, 3)),
            dma((2, 2, 3)),
            dma((2,)),
            dma((4,)),
            dma((2,)),
            dma((4,)),
            dma(()),
            dma(()),
            dma(()),
            dma((4,)),
            dma((2,)),
            dma((2,)),
            dma((2,)),
            dma(()),
            dma(()),
            dma((2,)),
            dma((2,)),
            dma((2,)),
            dma((3,)),
            dma((3,)),
            dma((8,)),
            dma((8,)),
            dma((8,)),
            dma((8,)),
            dma((8,)),
            dma((8,)),
            dma((8,)),
            dma((8,)),
            dma((8,)),
            dma((8,)),
            dma((8,)),
            dma((2,)),
            dma((2, 3)),
            dma((2, 3)),
            dma((3,)),
            dma((3,)),
            dma((7,)),
            dma(()),
        ],
        compiler_params=pltpu.CompilerParams(
            collective_id=0, has_side_effects=True, vmem_limit_bytes=60 << 20
        ),
    )(
        hidden[0],
        norm_gain,
        kv_weight,
        attn_flat,
        segment_ids,
        final_gain[None],
        reward_head[None],
    )
    rewards = stats[:, 4, 0] * lax.rsqrt(stats[:, 0, 0] / width + EPS)
    pair_loss = jnp.where(
        ranks[:, None] < ranks[None, :], jax.nn.softplus(rewards[None, :] - rewards[:, None]), 0.0
    )
    return (moved[None], rewards, pair_loss)


def shards(hidden, norm_gain, kv_weight, attn_flat, final_gain, reward_head, segment_ids, ranks):
    blocks = lax.axis_size("dp")
    lanes = lax.axis_size("mp")
    kv_local = kv_weight.shape[2] // (2 * HD)
    kept = (
        (lax.axis_size("section"), blocks, lanes, kv_local) == (2, 4, 4, 2)
        and hidden.shape[1:] == (128, 4096)
        and attn_flat.shape == (1, 1, 2097152)
    )
    args = (hidden, norm_gain, kv_weight, attn_flat, final_gain, reward_head, segment_ids, ranks)
    return (kept_shards if kept else gathered_shards)(*args)


def solution(mesh):
    placed = (
        P("section", "dp", None),
        P("section", None),
        P("section", None, "mp"),
        P("section", "mp", "dp"),
        P(),
        P(),
        P("section", None),
        P(),
    )
    return jax.shard_map(
        shards,
        mesh=mesh,
        in_specs=placed,
        out_specs=(P("section", "dp", None), P(), P()),
        check_vma=False,
    )
```

```python
import functools

import jax
import jax.numpy as jnp
from jax import lax
from jax.experimental import pallas as pl
from jax.experimental.pallas import tpu as pltpu
from jax.sharding import PartitionSpec as P

HD = 128
QH = 32
KVH = 8


EPS = 1e-05


def passed_along(block, axis, distance):
    devices = range(lax.axis_size(axis))
    route = [(i - distance, i) for i in devices if i - distance in devices]
    return lax.ppermute(block, axis, route)


def gathered_shards(hidden, norm_gain, kv_weight, attn_flat, final_gain, reward_head, segment_ids, ranks):
    state = hidden[0]
    tokens = state.shape[0]
    width = state.shape[1]
    seg_row = segment_ids[0]
    blocks = lax.axis_size("dp")
    block = lax.axis_index("dp")
    phases = lax.axis_size("section")
    phase_now = lax.axis_index("section")
    responses = ranks.shape[0]
    state_wide = state.astype(jnp.float32)
    normed = (
        state_wide
        * lax.rsqrt(jnp.mean(state_wide * state_wide, -1, keepdims=True) + EPS)
        * norm_gain[0]
    ).astype(jnp.bfloat16)
    keyval = jnp.dot(normed, kv_weight[0], preferred_element_type=jnp.float32).astype(jnp.bfloat16)
    kv_local = keyval.shape[1] // (2 * HD)
    group = QH // KVH
    q_width = kv_local * group * HD
    flat = lax.all_gather(attn_flat[0, 0], "dp", axis=0, tiled=True)
    w_query = flat[: width * q_width].reshape(width, q_width)
    w_out = flat[width * q_width : 2 * width * q_width].reshape(q_width, width)
    query = jnp.dot(normed, w_query, preferred_element_type=jnp.float32).astype(jnp.bfloat16)
    query = query.reshape(tokens, kv_local, group, HD)
    block_ids = jnp.arange(blocks, dtype=jnp.int32)
    own_seg = jnp.sum(jnp.where(block_ids == block, seg_row, 0))
    query_pos = block * tokens + jnp.arange(tokens, dtype=jnp.int32)
    piece = lax.all_gather(keyval, "dp", axis=0, tiled=True)
    peak = jnp.full((kv_local, group, tokens), -1e30, jnp.float32)
    count = piece.shape[0]
    key_pos = jnp.arange(count, dtype=jnp.int32)
    key_block = key_pos // tokens
    key_seg = jnp.sum(jnp.where(key_block[:, None] == block_ids[None, :], seg_row[None, :], 0), 1)
    parts = piece.reshape(count, kv_local, 2, HD)
    keys = parts[:, :, 0]
    values = parts[:, :, 1]
    earlier = (key_block < block) & (key_block >= 0) & ((key_seg == 0) | (key_seg == own_seg))
    same = (key_block == block)[None, :] & (key_pos[None, :] <= query_pos[:, None])
    visible = earlier[None, :] | same
    scores = jnp.einsum("tjgd,cjd->jgtc", query, keys, preferred_element_type=jnp.float32) * HD ** (
        -0.5
    )
    scores = jnp.where(visible[None, None], scores, -1e30)
    new_peak = jnp.maximum(peak, jnp.max(scores, -1))
    weights = jnp.where(visible[None, None], jnp.exp(scores - new_peak[..., None]), 0.0)
    total = jnp.sum(weights, -1)
    accum = jnp.einsum(
        "jgtc,cjd->jgtd", weights.astype(jnp.bfloat16), values, preferred_element_type=jnp.float32
    )
    peak, total, accum = (new_peak, total, accum)
    mixed = (
        (accum / total[..., None])
        .transpose(2, 0, 1, 3)
        .reshape(tokens, q_width)
        .astype(jnp.bfloat16)
    )
    partial_value = jnp.dot(mixed, w_out, preferred_element_type=jnp.float32)
    ends = (
        jnp.sum(
            (seg_row[None, :] <= jnp.arange(1, responses + 1, dtype=jnp.int32)[:, None]).astype(
                jnp.int32
            ),
            1,
        )
        - 1
    )
    at_end = (ends == block) & (phase_now == phases - 1)
    summed = lax.psum(partial_value.astype(jnp.bfloat16), "mp").astype(jnp.float32)
    updated = (state_wide + summed).astype(jnp.bfloat16)
    moved = passed_along(updated, "section", 1)
    last_row = updated[tokens - 1].astype(jnp.float32)
    squares = jnp.sum(last_row * last_row)
    product = jnp.sum(last_row * final_gain * reward_head)
    sums_sq, dots = lax.psum(
        (jnp.where(at_end, squares, 0.0), jnp.where(at_end, product, 0.0)), ("section", "dp")
    )
    rewards = dots * lax.rsqrt(sums_sq / width + EPS)
    pair_loss = jnp.where(
        ranks[:, None] < ranks[None, :], jax.nn.softplus(rewards[None, :] - rewards[:, None]), 0.0
    )
    return (moved[None], rewards, pair_loss)


BF = jnp.bfloat16
F32 = jnp.float32
HIDE = -1e30


def copy_to(src, dst, send, recv, **where):
    return pltpu.make_async_remote_copy(
        src_ref=src,
        dst_ref=dst,
        send_sem=send,
        recv_sem=recv,
        device_id=where,
        device_id_type=pl.DeviceIdType.MESH,
    )


def relay_kernel(
    h_ref,
    gain_ref,
    kvw_hbm,
    flat_hbm,
    seg_ref,
    fg_ref,
    rh_ref,
    out_ref,
    stat_ref,
    kvw,
    flat,
    wq,
    wo,
    nrm,
    xq,
    kvs,
    kvr,
    qs,
    qo,
    qr,
    mx,
    mr,
    osend,
    oown,
    orecv,
    ysend,
    yown,
    yrecv,
    zsend,
    zrecv,
    us,
    uin,
    hx,
    hrow,
    rx,
    rkv,
    qs1,
    qr1,
    osum,
    zin,
    psum,
    pin,
    st,
    sres,
    load_sem,
    adj_s,
    adj_r,
    pair_s,
    pair_r,
    far_s,
    far_r,
    sp_s,
    sp_r,
    row_s,
    row_r,
    kv_s,
    kv_r,
    hx_s,
    hx_r,
    hr_s,
    hr_r,
    rx_s,
    rx_r,
    rl_s,
    kx_s,
    kx_r,
    rk_s,
    w_s,
    w_r,
    p_s,
    p_r,
    q_s,
    q_r,
    m_s,
    m_r,
    o_s,
    o_r,
    y_s,
    y_r,
    z_s,
    z_r,
    u_s,
    u_r,
    f_s,
    f_r,
    st_s,
    st_r,
    sr_s,
    sr_r,
):
    s = lax.axis_index("section")
    d = lax.axis_index("dp")
    m = lax.axis_index("mp")
    y = m // 2
    c = m % 2
    across = (m + 2) % 4
    beside = m + 1 - 2 * c
    first_phase = s == 0
    last_phase = s == 1
    load_kv = pltpu.make_async_copy(kvw_hbm.at[0], kvw, load_sem.at[0])
    CH = 4
    SPAN = 2097152 // CH

    def load_flat(i):
        cut = slice(i * SPAN, (i + 1) * SPAN)
        return pltpu.make_async_copy(
            flat_hbm.at[:, :, cut], flat.at[:, :, cut], load_sem.at[1 + i]
        )

    @pl.when(d >= 2)
    def _():
        load_kv.start()

    for i in range(CH):
        load_flat(i).start()

    @pl.when(d < 2)
    def _():
        load_kv.start()

    barrier = pltpu.get_barrier_semaphore()
    for k in range(1, 4):
        pl.semaphore_signal(
            barrier, inc=1, device_id={"mp": (m + k) % 4}, device_id_type=pl.DeviceIdType.MESH
        )
    for k in range(1, 8):
        t = (s * 4 + d + k) % 8
        pl.semaphore_signal(
            barrier,
            inc=1,
            device_id={"section": t // 4, "dp": t % 4},
            device_id_type=pl.DeviceIdType.MESH,
        )
    h = h_ref[...].astype(F32)
    scale = lax.rsqrt(jnp.mean(h * h, -1, keepdims=True) + EPS)
    nrm[...] = (h * scale * gain_ref[...]).astype(BF)

    mine_out = pl.ds(pl.multiple_of((2 * c + y) * 1024, 1024), 1024)
    across_out = pl.ds(pl.multiple_of((2 * c + 1 - y) * 1024, 1024), 1024)

    natural = pl.ds(pl.multiple_of(m * 1024, 1024), 1024)

    def halves(t):
        return slice(t * 2048, (t + 1) * 2048)

    def keyval():
        load_kv.wait()
        for t in range(2):
            kvs[t] = jnp.dot(
                nrm[...], kvw[:, t * 256 : (t + 1) * 256], preferred_element_type=F32
            ).astype(BF)

            @pl.when(d == t)
            def _():
                kvr[t] = kvs[t]

    def shape_query():
        for i in range(CH):
            load_flat(i).wait()

            @pl.loop(0, 32 // CH)
            def _(k):
                k = k + i * (32 // CH)
                part = flat[0, :, pl.ds(pl.multiple_of(k * 65536, 65536), 65536)].astype(F32)
                wq[pl.ds(pl.multiple_of(k * 64, 64), 64), :] = part.reshape(64, 1024).astype(BF)

    def shape_out():
        for i in range(CH):
            load_flat(i).wait()

            @pl.loop(0, 32 // CH)
            def _(k):
                k = k + i * (32 // CH)
                part = flat[0, :, pl.ds(pl.multiple_of(k * 65536, 65536), 65536)].astype(F32)
                wo[pl.ds(pl.multiple_of(k * 16, 16), 16), :] = part.reshape(16, 4096).astype(BF)

    @pl.when(first_phase)
    def _():
        for t in range(2):

            @pl.when(d == t)
            def _():
                xq[t] = nrm[:, halves(t)]

    @pl.when(last_phase)
    def _():
        for b in range(4):
            for t in range(2):
                if b == t:

                    @pl.when(d == b)
                    def _():
                        xq[0, 16 * b : 16 * b + 16] = nrm[112:128, halves(t)]

    @pl.when(d < 2)
    def _():
        shape_query()

    pl.semaphore_wait(barrier, 10)

    def pair_rows(p):
        return pl.ds(pl.multiple_of(p * 64 + c * 32, 32), 32)

    def adj_send(p):
        rows = pair_rows(p)
        cols = pl.ds(pl.multiple_of((1 - d) * 2048, 2048), 2048)
        return copy_to(
            nrm.at[rows, cols], xq.at[d, rows], adj_s.at[p], adj_r.at[p], dp=1 - d
        )

    def adj_arrive(p):
        rows = pair_rows(p)
        return copy_to(
            xq.at[1 - d, rows], xq.at[1 - d, rows], adj_s.at[p], adj_r.at[p], dp=1 - d
        )

    def pair_copy(p):
        rows = pair_rows(p)
        return copy_to(
            xq.at[1 - d, rows], xq.at[1 - d, rows], pair_s.at[p], pair_r.at[p], mp=beside
        )

    def quarter(p, which):
        return pl.ds(pl.multiple_of(p * 64 + which * 16, 16), 16)

    def far_send(p):
        rows = quarter(p, m)
        return copy_to(
            nrm.at[rows, halves(1)], xq.at[d, rows], far_s.at[p], far_r.at[d - 2, p], dp=1
        )

    def far_zero(p):
        rows = quarter(p, m)
        return copy_to(
            nrm.at[rows, halves(0)], xq.at[d, rows], rx_s.at[p], far_r.at[d - 2, p], dp=0
        )

    def x_hop(p):
        return copy_to(
            nrm.at[quarter(p, m), halves(0)], rx.at[p], rx_s.at[p], rx_r.at[p], section=1
        )

    def x_relay(p):
        return pltpu.make_async_remote_copy(
            src_ref=rx.at[p],
            dst_ref=xq.at[d, quarter(p, m)],
            send_sem=rl_s.at[p],
            recv_sem=far_r.at[d - 2, p],
            device_id={"section": 0, "dp": 0},
            device_id_type=pl.DeviceIdType.MESH,
        )

    def kv_x():
        return copy_to(kvs, rkv, kx_s, kx_r, section=1)

    def kv_relay(t):
        return pltpu.make_async_remote_copy(
            src_ref=rkv.at[t],
            dst_ref=kvr.at[d],
            send_sem=rk_s.at[t],
            recv_sem=kv_r.at[d],
            device_id={"section": 0, "dp": t},
            device_id_type=pl.DeviceIdType.MESH,
        )

    def far_arrive(b, p):
        rows = quarter(p, m)
        return copy_to(
            xq.at[b, rows], xq.at[b, rows], far_s.at[p], far_r.at[b - 2, p], dp=b
        )

    def spread(b, p, k):
        rows = quarter(p, across if k == 2 else m)
        return copy_to(
            xq.at[b, rows],
            xq.at[b, rows],
            sp_s.at[b - 2, p, k],
            sp_r.at[b - 2, p, k],
            mp=across if k == 0 else beside,
        )

    def row_send(t):
        return copy_to(
            nrm.at[112:128, halves(t)],
            xq.at[0, pl.ds(pl.multiple_of(d * 16, 16), 16)],
            row_s.at[t],
            row_r.at[d],
            dp=t,
        )

    def row_arrive(b):
        rows = slice(16 * b, 16 * b + 16)
        return copy_to(xq.at[0, rows], xq.at[0, rows], row_s.at[0], row_r.at[b], dp=b)

    def kv_hop(t):
        return copy_to(kvs.at[t], kvr.at[d], kv_s.at[t], kv_r.at[d], dp=t)

    def kv_arrive(b):
        return copy_to(kvr.at[b], kvr.at[b], kv_s.at[0], kv_r.at[b], dp=b)

    def hx_copy():
        return copy_to(h_ref.at[:, mine_out], hx, hx_s, hx_r, section=1 - s)

    def hr_send():
        return copy_to(
            h_ref.at[112:128, natural],
            hrow.at[pl.ds(pl.multiple_of(d * 16, 16), 16)],
            hr_s,
            hr_r.at[d],
            dp=2,
        )

    def hr_arrive(b):
        rows = slice(16 * b, 16 * b + 16)
        return copy_to(hrow.at[rows], hrow.at[rows], hr_s, hr_r.at[b], dp=b)

    @pl.when(first_phase)
    def _():
        @pl.when(d < 2)
        def _():
            for p in range(2):
                adj_send(p).start()

        @pl.when(d == 2)
        def _():
            for p in range(2):
                far_send(p).start()
                far_zero(p).start()

    @pl.when(last_phase)
    def _():
        for t in range(2):

            @pl.when(d != t)
            def _():
                row_send(t).start()

    keyval()
    hops = (d < 2) | last_phase
    for t in range(2):

        @pl.when(hops & (d != t))
        def _():
            kv_hop(t).start()

    @pl.when((d >= 2) & first_phase)
    def _():
        kv_x().start()

        @pl.when(d == 3)
        def _():
            for p in range(2):
                far_send(p).start()
                far_zero(p).start()

    @pl.when(first_phase)
    def _():
        @pl.when(d < 2)
        def _():
            hx_copy().start()

        out_ref[...] = jnp.zeros_like(out_ref)

    @pl.when(last_phase)
    def _():
        @pl.when(d != 2)
        def _():
            hr_send().start()

        @pl.when(d == 2)
        def _():
            hrow[32:48] = h_ref[112:128, natural]

    def q_copy(g):
        return copy_to(qs.at[g], qr.at[g], q_s.at[g], q_r.at[g], dp=1 - d)

    def m_copy(g):
        return copy_to(mx.at[g], mr.at[g], m_s.at[g], m_r.at[g], dp=d + 2)

    def m_arrive(g):
        return copy_to(mr.at[g], mr.at[g], m_s.at[g], m_r.at[g], dp=d - 2)

    def w_query():
        return copy_to(qs1, qr1, w_s.at[0], w_r.at[0], dp=1 - d)

    def w_out():
        return copy_to(osum, zin, w_s.at[1], w_r.at[1], dp=5 - d)

    def project(g):
        b, rows = g // 2, slice(g % 2 * 64, g % 2 * 64 + 64)
        mine = pl.ds(pl.multiple_of(d * 512, 512), 512)
        other = pl.ds(pl.multiple_of((1 - d) * 512, 512), 512)
        qs[g] = jnp.dot(xq[b, rows], wq[:, other], preferred_element_type=F32).astype(BF)
        q_copy(g).start()
        qo[g] = jnp.dot(xq[b, rows], wq[:, mine], preferred_element_type=F32)

    def attend(g, blocks, mask):
        q_copy(g).wait_recv()
        mix(g, qo[g] + qr[g].astype(F32), blocks, mask)

        m_copy(g).start()

    def mix(g, q, blocks, mask):
        q = q.astype(BF)
        q = jnp.concatenate([q[:, j * HD : (j + 1) * HD] for j in range(4)], 0)
        scores = []
        for j in range(blocks):
            score = (
                lax.dot_general(
                    q, kvr[j, :, :HD], (((1,), (1,)), ((), ())), preferred_element_type=F32
                )
                * HD ** (-0.5)
            )
            scores.append(mask(j, score))
        peak = functools.reduce(jnp.maximum, [jnp.max(x, -1, keepdims=True) for x in scores])
        total = jnp.zeros_like(peak)
        mixed = jnp.zeros((256, HD), F32)
        for j in range(blocks):
            weight = jnp.exp(scores[j] - peak)
            total = total + jnp.sum(weight, -1, keepdims=True)
            mixed = mixed + jnp.dot(
                weight.astype(BF), kvr[j, :, HD:], preferred_element_type=F32
            )
        mixed = (mixed / total).astype(BF)
        for j in range(4):
            mx[g, :, j * HD : (j + 1) * HD] = mixed[j * 64 : (j + 1) * 64]

    def block_mask(g):
        b, half = g // 2, g % 2

        def mask(j, score):
            if j < b:
                seen = (seg_ref[0, j] == 0) | (seg_ref[0, j] == seg_ref[0, b])
                return score + jnp.where(seen, 0.0, HIDE)
            row = lax.broadcasted_iota(jnp.int32, score.shape, 0) % 64 + half * 64
            col = lax.broadcasted_iota(jnp.int32, score.shape, 1)
            return jnp.where(col <= row, score, HIDE)

        return mask

    def ends_mask(j, score):
        row = lax.broadcasted_iota(jnp.int32, score.shape, 0) % 64
        col = lax.broadcasted_iota(jnp.int32, score.shape, 1)
        of = row // 16
        own = jnp.zeros_like(row)
        for b in range(4):
            own = own + jnp.where(of == b, seg_ref[0, b], 0)
        earlier = (of > j) & ((own == seg_ref[0, j]) | (seg_ref[0, j] == 0))
        same = (of == j) & (col <= row % 16 + 112)
        return jnp.where(earlier | same, score, HIDE)

    @pl.when((d < 2) & first_phase)
    def _():
        def adjacent(p):
            adj_arrive(p).wait_recv()
            pair_copy(p).start()

        def joined(p):
            pair_copy(p).wait_recv()

        def receive(b, p):
            far_arrive(b, p).wait_recv()
            spread(b, p, 0).start()
            spread(b, p, 1).start()

        def forward(b, p):
            spread(b, p, 0).wait_recv()
            spread(b, p, 2).start()

        def complete(b, p):
            spread(b, p, 1).wait_recv()
            spread(b, p, 2).wait_recv()

        def keys(b):
            @pl.when(d != b)
            def _():
                kv_arrive(b).wait_recv()

        def paired(g):
            @pl.when(d != g // 2)
            def _():
                joined(g % 2)

        adjacent(0)
        paired(0)
        project(0)
        adjacent(1)
        paired(1)
        project(1)
        keys(0)
        attend(0, 1, block_mask(0))
        paired(2)
        project(2)
        receive(2, 0)
        attend(1, 1, block_mask(1))
        receive(2, 1)
        paired(3)
        project(3)
        keys(1)
        forward(2, 0)
        attend(2, 2, block_mask(2))
        receive(3, 0)
        forward(2, 1)
        complete(2, 0)
        project(4)
        receive(3, 1)
        attend(3, 2, block_mask(3))
        complete(2, 1)
        project(5)
        forward(3, 0)
        keys(2)
        attend(4, 3, block_mask(4))
        forward(3, 1)
        complete(3, 0)
        project(6)
        attend(5, 3, block_mask(5))
        complete(3, 1)
        project(7)
        keys(3)
        attend(6, 4, block_mask(6))
        attend(7, 4, block_mask(7))

    @pl.when((d < 2) & last_phase)
    def _():
        for b in range(4):

            @pl.when(d != b)
            def _():
                row_arrive(b).wait_recv()

        mine = pl.ds(pl.multiple_of(d * 512, 512), 512)
        other = pl.ds(pl.multiple_of((1 - d) * 512, 512), 512)
        qs1[...] = jnp.dot(xq[0, 0:64], wq[:, other], preferred_element_type=F32)
        w_query().start()
        own = jnp.dot(xq[0, 0:64], wq[:, mine], preferred_element_type=F32)
        for b in range(4):

            @pl.when(d != b)
            def _():
                kv_arrive(b).wait_recv()

        w_query().wait_recv()
        mix(0, own + qr1[...], 4, ends_mask)
        m_copy(0).start()

    def o_copy(g):
        return copy_to(osend.at[g], orecv.at[g], o_s.at[g], o_r.at[g], mp=beside)

    def y_copy(g):
        return copy_to(ysend.at[g], yrecv.at[g], y_s.at[g], y_r.at[g], mp=across)

    def z_copy(g):
        return copy_to(zsend.at[g], zrecv.at[g], z_s.at[g], z_r.at[g], dp=5 - d)

    def u_copy(g):
        return pltpu.make_async_remote_copy(
            src_ref=us.at[g],
            dst_ref=uin.at[g % 2],
            send_sem=u_s.at[g],
            recv_sem=u_r.at[g % 2],
            device_id={"section": 1, "dp": g // 2},
            device_id_type=pl.DeviceIdType.MESH,
        )

    def keeper(g):
        return 3 if g >= 6 else 2

    def first(g):
        m_arrive(g).wait_recv()
        mine = pl.ds(pl.multiple_of(c * 2048, 2048), 2048)
        other = pl.ds(pl.multiple_of((1 - c) * 2048, 2048), 2048)
        osend[g] = jnp.dot(mr[g], wo[:, other], preferred_element_type=F32).astype(BF)
        o_copy(g).start()
        oown[g] = jnp.dot(mr[g], wo[:, mine], preferred_element_type=F32)

    def second(g):
        o_copy(g).wait_recv()
        mine = pl.ds(pl.multiple_of(y * 1024, 1024), 1024)
        other = pl.ds(pl.multiple_of((1 - y) * 1024, 1024), 1024)
        ysend[g] = (oown[g, :, other] + orecv[g, :, other].astype(F32)).astype(BF)
        y_copy(g).start()
        yown[g] = oown[g, :, mine] + orecv[g, :, mine].astype(F32)

    def third(g):
        y_copy(g).wait_recv()

        @pl.when(d != keeper(g))
        def _():
            zsend[g] = (yown[g] + yrecv[g].astype(F32)).astype(BF)
            z_copy(g).start()

        @pl.when(d == keeper(g))
        def _():
            yown[g] = yown[g] + yrecv[g].astype(F32)

    def fourth(g):
        @pl.when(d == keeper(g))
        def _():
            z_copy(g).wait_recv()
            us[g] = (yown[g] + zrecv[g].astype(F32)).astype(BF)
            u_copy(g).start()

    @pl.when((d >= 2) & last_phase)
    def _():
        copy_to(rkv, rkv, kx_s, kx_r, section=0).wait_recv()
        for t in (1, 0):
            kv_relay(t).start()

    @pl.when(d >= 2)
    def _():
        shape_out()

        @pl.when(first_phase)
        def _():
            hx_copy().start()

    @pl.when((d >= 2) & first_phase)
    def _():
        for g in range(13):
            if g < 8:
                first(g)
            if 0 <= g - 3 < 8:
                third(g - 3)
            if 0 <= g - 5 < 8:
                fourth(g - 5)
            if g < 8:
                second(g)

    def st_copy(k):
        t = (m + k) % 4
        return copy_to(st.at[m], st.at[m], st_s.at[k - 1], st_r.at[k - 1], mp=t)

    def st_arrive(k):
        t = (m + 4 - k) % 4
        return copy_to(st.at[t], st.at[t], st_s.at[k - 1], st_r.at[k - 1], mp=t)

    def sr_copy(k):
        t = (6 + k) % 8
        return pltpu.make_async_remote_copy(
            src_ref=sres,
            dst_ref=sres,
            send_sem=sr_s.at[k - 1],
            recv_sem=sr_r,
            device_id={"section": t // 4, "dp": t % 4},
            device_id_type=pl.DeviceIdType.MESH,
        )

    def p_copy(k):
        t = (m + k) % 4
        return copy_to(psum.at[t], pin.at[m], p_s.at[k - 1], p_r.at[k - 1], mp=t)

    def p_arrive(k):
        t = (m + 4 - k) % 4
        return copy_to(pin.at[t], pin.at[t], p_s.at[k - 1], p_r.at[k - 1], mp=t)

    def last_rows(a):
        rest = jnp.zeros((4, a.shape[1]), F32)
        return jnp.concatenate([a[16 * b + 15 : 16 * b + 16] for b in range(4)] + [rest], 0)

    @pl.when((d >= 2) & last_phase)
    def _():
        m_arrive(0).wait_recv()
        for k in range(4):
            cols = slice(k * 1024, k * 1024 + 1024)
            osum[:, cols] = last_rows(jnp.dot(mr[0], wo[:, cols], preferred_element_type=F32))

        @pl.when(d == 3)
        def _():
            w_out().start()

    @pl.when((d == 2) & last_phase)
    def _():
        for b in (0, 1, 3):
            hr_arrive(b).wait_recv()
        w_out().wait_recv()
        for k in range(4):
            cols = slice(k * 1024, k * 1024 + 1024)
            psum[k] = (osum[:, cols] + zin[:, cols]).astype(BF).astype(F32)
        pin[m] = psum[m]
        for k in range(1, 4):
            p_copy(k).start()
        for k in range(1, 4):
            p_arrive(k).wait_recv()
        total = (pin[0] + pin[1]) + (pin[2] + pin[3])
        v = (last_rows(hrow[...].astype(F32)) + total).astype(BF).astype(F32)
        squares = jnp.sum(v * v, -1, keepdims=True)
        product = jnp.sum(v * fg_ref[:, natural] * rh_ref[:, natural], -1, keepdims=True)
        spot = lax.broadcasted_iota(jnp.int32, squares.shape, 0)
        half = lax.broadcasted_iota(jnp.int32, (8, 128), 0) < 4
        for r in range(sres.shape[0]):
            end = -1
            for b in range(4):
                end = end + jnp.where(seg_ref[0, b] <= r + 1, 1, 0)
            here = spot == end
            one = jnp.sum(jnp.where(here, squares, 0.0), keepdims=True)
            two = jnp.sum(jnp.where(here, product, 0.0), keepdims=True)
            st[m, r] = jnp.where(half, one, two)
        for k in range(1, 4):
            st_copy(k).start()
        for k in range(1, 4):
            st_arrive(k).wait_recv()
        sres[...] = (st[0] + st[1]) + (st[2] + st[3])
        for k in range(1, 8):
            sr_copy(k).start()

    @pl.when(last_phase)
    def _():
        def f_copy(p, k):
            rows = slice(p * 64, p * 64 + 64)
            cols = across_out if k == 2 else mine_out
            return copy_to(
                out_ref.at[rows, cols],
                out_ref.at[rows, cols],
                f_s.at[p, k],
                f_r.at[p, k],
                mp=across if k == 0 else beside,
            )

        def u_arrive(p):
            return copy_to(uin.at[p], uin.at[p], u_s.at[p], u_r.at[p], section=0)

        copy_to(hx, hx, hx_s, hx_r, section=0).wait_recv()
        for p in range(2):
            rows = slice(p * 64, p * 64 + 64)
            u_arrive(p).wait_recv()
            out_ref[rows, mine_out] = (
                hx[rows].astype(F32) + uin[p].astype(F32)
            ).astype(BF)
            f_copy(p, 0).start()
            f_copy(p, 1).start()
        for p in range(2):
            f_copy(p, 0).wait_recv()
            f_copy(p, 2).start()
        for p in range(2):
            f_copy(p, 1).wait_recv()
            f_copy(p, 2).wait_recv()
        for p in range(2):
            for k in range(3):
                f_copy(p, k).wait_send()

    leader = (d == 2) & last_phase

    @pl.when(jnp.logical_not(leader))
    def _():
        sr_copy(1).wait_recv()

    stat_ref[...] = sres[...]

    @pl.when(leader)
    def _():
        for k in range(1, 4):
            st_copy(k).wait_send()
        for k in range(1, 8):
            sr_copy(k).wait_send()

    for t in range(2):

        @pl.when(hops & (d != t))
        def _():
            kv_hop(t).wait_send()

            @pl.when(last_phase)
            def _():
                row_send(t).wait_send()

    @pl.when(first_phase)
    def _():
        hx_copy().wait_send()

        @pl.when(d < 2)
        def _():
            for p in range(2):
                adj_send(p).wait_send()
                pair_copy(p).wait_send()
                for b in (2, 3):
                    for k in range(3):
                        spread(b, p, k).wait_send()
            for g in range(8):
                q_copy(g).wait_send()
                m_copy(g).wait_send()

        @pl.when(d >= 2)
        def _():
            kv_x().wait_send()
            for p in range(2):
                far_zero(p).wait_send()
                far_send(p).wait_send()
            for g in range(8):
                o_copy(g).wait_send()
                y_copy(g).wait_send()

                @pl.when(d != keeper(g))
                def _():
                    z_copy(g).wait_send()

                @pl.when(d == keeper(g))
                def _():
                    u_copy(g).wait_send()

    @pl.when(last_phase)
    def _():
        @pl.when(d != 2)
        def _():
            hr_send().wait_send()

        @pl.when(d < 2)
        def _():
            w_query().wait_send()
            m_copy(0).wait_send()

        @pl.when(d == 3)
        def _():
            w_out().wait_send()

        @pl.when(d == 2)
        def _():
            for k in range(1, 4):
                p_copy(k).wait_send()

        @pl.when(d >= 2)
        def _():
            for p in range(2):
                kv_relay(p).wait_send()


def kept_shards(hidden, norm_gain, kv_weight, attn_flat, final_gain, reward_head, segment_ids, ranks):
    width = hidden.shape[2]
    responses = ranks.shape[0]
    vmem = pl.BlockSpec(memory_space=pltpu.VMEM)
    anywhere = pl.BlockSpec(memory_space=pl.ANY)
    dma = pltpu.SemaphoreType.DMA
    V = pltpu.VMEM
    moved, stats = pl.pallas_call(
        relay_kernel,
        out_shape=(
            jax.ShapeDtypeStruct((128, 4096), BF),
            jax.ShapeDtypeStruct((responses, 8, 128), F32),
        ),
        in_specs=[
            vmem,
            vmem,
            anywhere,
            anywhere,
            pl.BlockSpec(memory_space=pltpu.SMEM),
            vmem,
            vmem,
        ],
        out_specs=(vmem, vmem),
        scratch_shapes=[
            V((4096, 512), BF),
            V((1, 1, 2097152), BF),
            V((2048, 1024), BF),
            V((512, 4096), BF),
            V((128, 4096), BF),
            V((4, 128, 2048), BF),
            V((2, 128, 256), BF),
            V((4, 128, 256), BF),
            V((8, 64, 512), BF),
            V((8, 64, 512), F32),
            V((8, 64, 512), BF),
            V((8, 64, 512), BF),
            V((8, 64, 512), BF),
            V((8, 64, 2048), BF),
            V((8, 64, 2048), F32),
            V((8, 64, 2048), BF),
            V((8, 64, 1024), BF),
            V((8, 64, 1024), F32),
            V((8, 64, 1024), BF),
            V((8, 64, 1024), BF),
            V((8, 64, 1024), BF),
            V((8, 64, 1024), BF),
            V((2, 64, 1024), BF),
            V((128, 1024), BF),
            V((64, 1024), BF),
            V((2, 16, 2048), BF),
            V((2, 128, 256), BF),
            V((64, 512), F32),
            V((64, 512), F32),
            V((8, 4096), F32),
            V((8, 4096), F32),
            V((4, 8, 1024), F32),
            V((4, 8, 1024), F32),
            V((4, responses, 8, 128), F32),
            V((responses, 8, 128), F32),
            dma((5,)),
            dma((2,)),
            dma((2,)),
            dma((2,)),
            dma((2,)),
            dma((2,)),
            dma((2, 2)),
            dma((2, 2, 3)),
            dma((2, 2, 3)),
            dma((2,)),
            dma((4,)),
            dma((2,)),
            dma((4,)),
            dma(()),
            dma(()),
            dma(()),
            dma((4,)),
            dma((2,)),
            dma((2,)),
            dma((2,)),
            dma(()),
            dma(()),
            dma((2,)),
            dma((2,)),
            dma((2,)),
            dma((3,)),
            dma((3,)),
            dma((8,)),
            dma((8,)),
            dma((8,)),
            dma((8,)),
            dma((8,)),
            dma((8,)),
            dma((8,)),
            dma((8,)),
            dma((8,)),
            dma((8,)),
            dma((8,)),
            dma((2,)),
            dma((2, 3)),
            dma((2, 3)),
            dma((3,)),
            dma((3,)),
            dma((7,)),
            dma(()),
        ],
        compiler_params=pltpu.CompilerParams(
            collective_id=0, has_side_effects=True, vmem_limit_bytes=60 << 20
        ),
    )(
        hidden[0],
        norm_gain,
        kv_weight,
        attn_flat,
        segment_ids,
        final_gain[None],
        reward_head[None],
    )
    rewards = stats[:, 4, 0] * lax.rsqrt(stats[:, 0, 0] / width + EPS)
    pair_loss = jnp.where(
        ranks[:, None] < ranks[None, :], jax.nn.softplus(rewards[None, :] - rewards[:, None]), 0.0
    )
    return (moved[None], rewards, pair_loss)


def shards(hidden, norm_gain, kv_weight, attn_flat, final_gain, reward_head, segment_ids, ranks):
    blocks = lax.axis_size("dp")
    lanes = lax.axis_size("mp")
    kv_local = kv_weight.shape[2] // (2 * HD)
    kept = (
        (lax.axis_size("section"), blocks, lanes, kv_local) == (2, 4, 4, 2)
        and hidden.shape[1:] == (128, 4096)
        and attn_flat.shape == (1, 1, 2097152)
    )
    args = (hidden, norm_gain, kv_weight, attn_flat, final_gain, reward_head, segment_ids, ranks)
    return (kept_shards if kept else gathered_shards)(*args)


def solution(mesh):
    placed = (
        P("section", "dp", None),
        P("section", None),
        P("section", None, "mp"),
        P("section", "mp", "dp"),
        P(),
        P(),
        P("section", None),
        P(),
    )
    return jax.shard_map(
        shards,
        mesh=mesh,
        in_specs=placed,
        out_specs=(P("section", "dp", None), P(), P()),
        check_vma=False,
    )
```
